256 devices in a mesh: row: 16 (over z, core), col: 16 (over y, x).
Axes of the slice: x: 4, y: 4, z: 8, core: 2. Of those that a mesh axis runs over, the one named last changes fastest.
Arguments:
- tiles: bfloat16 [16, 16, 16, 512, 512], P('row', 'col'), as said below
- tile_rows: int32 [16, 16, 16], P('row', 'col'), may hold values from 0 to 11, as said below
- tile_cols: int32 [16, 16, 16], P('row', 'col'), may hold values from 0 to 11
- tile_counts: int32 [16, 16], P('row', 'col'), may hold values from 4 to 16, as said below
- sketch: bfloat16 [98304, 256], P(('row', 'col')), as said below
Outputs:
- basis: float32 [98304, 256], P(('row', 'col'))
- factor: float32 [256, 256], replicated
The draws below stay inside these ranges and needn't reach their ends.
Inputs may be any that keep to these rules, and one draw needn't show every extreme that they name: Within one device's slots the pairs (tile_rows, tile_cols) are all different. `tile_counts`: some device uses all 16 slots in every draw. `tiles`: real valued tile entries of order one over the square root of a row's fan-in. `sketch`: real valued entries of order one.
All inputs are finite; a program needn't handle non-finite values.
Results may differ from the reference program's by a relative error of at most 0.0023.
Values may be sent and summed in bfloat16 or wider, within the bound.
A program may use at most 64 MiB of HBM per device.

```python
import math
import jax
import jax.numpy as jnp
from jax import lax

TILE = 512
K = 256
BR = 12
BC = 12
CAP = 16
ROW_GROUPS = 16
COL_GROUPS = 16
ROWS = 98304
COLS = 98304


def draw_tiles(key, part):
    shape = (ROW_GROUPS, COL_GROUPS, CAP, TILE, TILE)
    noise_key, scale_key = jax.random.split(jax.random.fold_in(key, 11))
    values = jnp.clip(jax.random.normal(noise_key, shape, jnp.float32), -5.0, 5.0)
    row_scale = jnp.exp(jax.random.uniform(scale_key, (ROW_GROUPS, COL_GROUPS, CAP, TILE, 1), jnp.float32, 0.0, math.log(10.0)))
    fan_width = TILE * CAP * COL_GROUPS // BR
    return (values * row_scale / (4.6 * math.sqrt(fan_width))).astype(jnp.bfloat16)


def tile_layout(key):
    device_keys = jax.random.split(jax.random.fold_in(key, 5), ROW_GROUPS * COL_GROUPS)
    orders = jax.vmap(lambda one_key: jax.random.permutation(one_key, BR * BC))(device_keys)[:, :CAP]
    return orders.reshape(ROW_GROUPS, COL_GROUPS, CAP).astype(jnp.int32)


def draw_tile_rows(key, part):
    return tile_layout(key) // BC


def draw_tile_cols(key, part):
    return tile_layout(key) % BC


def draw_tile_counts(key, part):
    count_key, pick_key = jax.random.split(jax.random.fold_in(key, 17))
    counts = jax.random.randint(count_key, (ROW_GROUPS * COL_GROUPS,), max(1, CAP // 4), CAP + 1, jnp.int32)
    chosen = jax.random.randint(pick_key, (), 0, ROW_GROUPS * COL_GROUPS, jnp.int32)
    counts = counts.at[chosen].set(CAP)
    return counts.reshape(ROW_GROUPS, COL_GROUPS)


def draw_sketch(key, part):
    noise_key, scale_key = jax.random.split(jax.random.fold_in(key, 23), 2)
    column_scale = jnp.exp(jax.random.uniform(scale_key, (1, K), jnp.float32, 0.0, math.log(10.0)))
    values = jnp.clip(jax.random.normal(noise_key, (ROWS, K), jnp.float32), -5.0, 5.0)
    return (values * column_scale / 4.6).astype(jnp.bfloat16)


def setup_inputs(seed: int = 0) -> dict:
    seeds = jax.random.split(jax.random.key(seed), 6)
    tiles = draw_tiles(jax.random.fold_in(seeds[5], 71), 0)
    tile_rows = draw_tile_rows(jax.random.fold_in(seeds[5], 71), 0)
    tile_cols = draw_tile_cols(jax.random.fold_in(seeds[5], 71), 0)
    tile_counts = draw_tile_counts(jax.random.fold_in(seeds[5], 71), 0)
    sketch = draw_sketch(jax.random.fold_in(seeds[5], 71), 0)
    return {"tiles": tiles, "tile_rows": tile_rows, "tile_cols": tile_cols, "tile_counts": tile_counts, "sketch": sketch}


def reference(tiles, tile_rows, tile_cols, tile_counts, sketch):
    tile_size = tiles.shape[-1]
    sketch_width = sketch.shape[1]
    slot_count = tiles.shape[2]
    group_cols = tiles.shape[1]
    flat_tiles = tiles.reshape(-1, tile_size, tile_size)
    tile_total = flat_tiles.shape[0]
    rows_flat = tile_rows.reshape(-1).astype(jnp.int32)
    cols_flat = tile_cols.reshape(-1).astype(jnp.int32)
    counts = tile_counts.reshape(-1).astype(jnp.int32)

    def coords(position):
        position = position.astype(jnp.int32)
        device = position // slot_count
        slot_number = position % slot_count
        row_group = device // group_cols
        col_group = device % group_cols
        live_mask = (slot_number < counts[device]).astype(jnp.float32)
        row_start = ((row_group * BR + rows_flat[position]) * tile_size).astype(jnp.int32)
        col_start = ((col_group * BC + cols_flat[position]) * tile_size).astype(jnp.int32)
        matrix = lax.dynamic_index_in_dim(flat_tiles, position, 0, keepdims=False)
        return (matrix, live_mask, row_start, col_start)

    def first_pass(position, running):
        matrix, live_mask, row_start, col_start = coords(position)
        sketch_block = lax.dynamic_slice_in_dim(sketch, row_start, tile_size, 0)
        product = lax.dot_general(matrix.astype(jnp.float32), sketch_block.astype(jnp.float32), (((0,), (0,)), ((), ())), preferred_element_type=jnp.float32)
        current = lax.dynamic_slice_in_dim(running, col_start, tile_size, 0)
        return lax.dynamic_update_slice_in_dim(running, current + product * live_mask, col_start, 0)
    column_sum = lax.fori_loop(0, tile_total, first_pass, jnp.zeros((COLS, sketch_width), jnp.float32))
    columns = column_sum.astype(jnp.bfloat16)

    def second_pass(position, running):
        matrix, live_mask, row_start, col_start = coords(position)
        column_block = lax.dynamic_slice_in_dim(columns, col_start, tile_size, 0)
        product = jnp.dot(matrix.astype(jnp.float32), column_block.astype(jnp.float32), preferred_element_type=jnp.float32)
        current = lax.dynamic_slice_in_dim(running, row_start, tile_size, 0)
        return lax.dynamic_update_slice_in_dim(running, current + product * live_mask, row_start, 0)
    new_sketch = lax.fori_loop(0, tile_total, second_pass, jnp.zeros((ROWS, sketch_width), jnp.float32))
    gram_matrix = jnp.dot(new_sketch.T.astype(jnp.float32), new_sketch.astype(jnp.float32), precision=lax.Precision.HIGHEST, preferred_element_type=jnp.float32) / ROWS
    cholesky_lower = jnp.linalg.cholesky(gram_matrix)
    basis_rows = lax.linalg.triangular_solve(cholesky_lower, new_sketch, left_side=False, lower=True, transpose_a=True)
    return (basis_rows, cholesky_lower.T)
```

```python
import functools

import jax
import jax.numpy as jnp
from jax import lax
from jax.experimental import pallas as pl
from jax.experimental.pallas import tpu as pltpu
from jax.sharding import PartitionSpec as P

TILE = 512
K = 256
BR = 12
BC = 12
CAP = 16
SHARD = 384
FULL = 6144
ROWS = 98304
MESH = pl.DeviceIdType.MESH
HI = lax.Precision.HIGHEST
VMEM_LIMIT = 60 * 1024 * 1024


def vmem(shape, dtype):
    return pltpu.VMEM(shape, dtype)


def whole():
    return pl.BlockSpec(memory_space=pltpu.VMEM)


def flip(i, g):
    x, y = lax.rem(i, 4), lax.div(i, 4)
    if g == 0:
        return i + 1 - 2 * lax.rem(x, 2)
    if g == 1:
        return i + 3 - 2 * x
    if g == 2:
        return i + 4 - 8 * lax.rem(y, 2)
    return i + 12 - 8 * y


def greet(devices):
    barrier = pltpu.get_barrier_semaphore()
    for device in devices:
        pl.semaphore_signal(barrier, inc=1, device_id=device, device_id_type=MESH)
    pl.semaphore_wait(barrier, len(devices))


def remote(src, dst, send_sem, recv_sem, device):
    return pltpu.make_async_remote_copy(
        src_ref=src,
        dst_ref=dst,
        send_sem=send_sem,
        recv_sem=recv_sem,
        device_id=device,
        device_id_type=MESH,
    )


def rows_at(start, size, step):
    return pl.ds(pl.multiple_of(start, step), size)


AG_STREAMS = 8
AG_Q = SHARD // AG_STREAMS


def sketch_gather(shard_ref, out_ref, send_sem, recv_sem):
    row, me = lax.axis_index("row"), lax.axis_index("col")
    near = [(row, flip(me, g)) for g in range(4)]
    greet(near)
    out_ref[rows_at(me * SHARD, SHARD, SHARD), :] = shard_ref[...]
    held = [[me] for _ in range(AG_STREAMS)]
    pending = [[] for _ in range(AG_STREAMS)]
    every = []
    for step in range(4):
        for k in range(AG_STREAMS):
            g = (k + step) % 4
            for copy in pending[k]:
                copy.wait_recv()
            pending[k] = []
            for n, block in enumerate(held[k]):
                at = rows_at(block * SHARD + k * AG_Q, AG_Q, 16)
                src = shard_ref.at[pl.ds(k * AG_Q, AG_Q), :] if n == 0 else out_ref.at[at, :]
                slot = k * 15 + 2**step - 1 + n
                copy = remote(src, out_ref.at[at, :], send_sem.at[slot], recv_sem.at[slot], near[g])
                copy.start()
                pending[k].append(copy)
                every.append(copy)
            held[k] = held[k] + [flip(b, g) for b in held[k]]
    for k in range(AG_STREAMS):
        for copy in pending[k]:
            copy.wait_recv()
    for copy in every:
        copy.wait_send()


def gather_sketch(sketch):
    return pl.pallas_call(
        sketch_gather,
        out_shape=jax.ShapeDtypeStruct((FULL, K), jnp.bfloat16),
        in_specs=[whole()],
        out_specs=whole(),
        scratch_shapes=[
            pltpu.SemaphoreType.DMA((AG_STREAMS * 15,)),
            pltpu.SemaphoreType.DMA((AG_STREAMS * 15,)),
        ],
        compiler_params=pltpu.CompilerParams(
            collective_id=0, has_side_effects=True, vmem_limit_bytes=VMEM_LIMIT
        ),
        name="gather_sketch",
    )(sketch)


def tile_loop(transposed, rows_ref, cols_ref, count_ref, tile_ref, in_ref, out_ref, acc_ref):
    s = pl.program_id(0)

    @pl.when(s == 0)
    def _():
        acc_ref[...] = jnp.zeros_like(acc_ref)

    @pl.when(s < count_ref[0])
    def _():
        r, c = rows_ref[s], cols_ref[s]
        src, dst = (r, c) if transposed else (c, r)
        block = in_ref[pl.ds(pl.multiple_of(src * TILE, TILE), TILE), :]
        dims = (((0,), (0,)), ((), ())) if transposed else (((1,), (0,)), ((), ()))
        product = lax.dot_general(tile_ref[0], block, dims, preferred_element_type=jnp.float32)
        at = pl.ds(pl.multiple_of(dst * TILE, TILE), TILE)
        acc_ref[at, :] = acc_ref[at, :] + product

    @pl.when(s == CAP - 1)
    def _():
        out_ref[...] = acc_ref[...].astype(out_ref.dtype)


def tile_loop_f32(transposed, rows_ref, cols_ref, count_ref, tile_ref, in_ref, out_ref):
    s = pl.program_id(0)

    @pl.when(s == 0)
    def _():
        out_ref[...] = jnp.zeros_like(out_ref)

    @pl.when(s < count_ref[0])
    def _():
        r, c = rows_ref[s], cols_ref[s]
        src, dst = (r, c) if transposed else (c, r)
        block = in_ref[pl.ds(pl.multiple_of(src * TILE, TILE), TILE), :]
        dims = (((0,), (0,)), ((), ())) if transposed else (((1,), (0,)), ((), ()))
        product = lax.dot_general(tile_ref[0], block, dims, preferred_element_type=jnp.float32)
        at = pl.ds(pl.multiple_of(dst * TILE, TILE), TILE)
        out_ref[at, :] = out_ref[at, :] + product


def multiply(transposed, dtype, tiles, rows, cols, count, operand):
    f32 = dtype == jnp.float32
    body = tile_loop_f32 if f32 else tile_loop

    def tile_at(s, rows_ref, cols_ref, count_ref):
        return (jnp.minimum(s, count_ref[0] - 1), 0, 0)

    return pl.pallas_call(
        functools.partial(body, transposed),
        out_shape=jax.ShapeDtypeStruct((FULL, K), dtype),
        grid_spec=pltpu.PrefetchScalarGridSpec(
            num_scalar_prefetch=3,
            grid=(CAP,),
            in_specs=[
                pl.BlockSpec((1, TILE, TILE), tile_at),
                pl.BlockSpec((FULL, K), lambda *_: (0, 0), pipeline_mode=pl.Buffered(1)),
            ],
            out_specs=pl.BlockSpec((FULL, K), lambda *_: (0, 0), pipeline_mode=pl.Buffered(1)),
            scratch_shapes=[] if f32 else [vmem((FULL, K), jnp.float32)],
        ),
        compiler_params=pltpu.CompilerParams(
            dimension_semantics=("arbitrary",), vmem_limit_bytes=VMEM_LIMIT
        ),
        name="tiles_t" if transposed else "tiles_n",
    )(rows, cols, count, tiles, operand)


HALF = SHARD // 2
CHAINS = ((1, 0, 4), (-1, 1, 4), (1, 1, 3), (-1, 0, 3))


def column_exchange(
    part_ref, out_ref, pair_buf, sums, landed, pair_send, pair_recv, chain_send, chain_recv,
    own_buf, gather_send, gather_recv, twin_send, twin_recv,
):
    row, col = lax.axis_index("row"), lax.axis_index("col")
    z, core = lax.div(row, 2), lax.rem(row, 2)
    twin = (row + 1 - 2 * core, col)

    def ring(d):
        return lax.rem(z + d + 8, 8)

    side = {1: (2 * ring(1) + core, col), -1: (2 * ring(-1) + core, col)}
    greet([twin, side[1], side[-1]])

    order = []
    for t in range(1, 5):
        for direction, half, hops in CHAINS:
            if t <= hops:
                d = direction * (hops + 1 - t)
                order.append((d % 8, half))
    order += [(0, 0), (0, 1)]
    seen = []
    for item in order:
        if item not in seen:
            seen.append(item)
    pair = {}
    for n, (d, half) in enumerate(seen):
        slot = d * 2 + half
        theirs = rows_at((2 * ring(d) + 1 - core) * SHARD + half * HALF, HALF, HALF)
        pair[(d, half)] = remote(
            part_ref.at[theirs, :], pair_buf.at[slot], pair_send.at[slot], pair_recv.at[slot], twin
        )
        pair[(d, half)].start()
    done = set()

    def chip_sum(d, half):
        d = d % 8
        slot = d * 2 + half
        if (d, half) not in done:
            pair[(d, half)].wait_recv()
            done.add((d, half))
        mine = rows_at((2 * ring(d) + core) * SHARD + half * HALF, HALF, HALF)
        return part_ref[mine, :] + pair_buf[slot]

    last = {}
    sends = []
    for t in range(1, 5):
        for n, (direction, half, hops) in enumerate(CHAINS):
            if t > hops:
                continue
            slot = n * 4 + t - 1
            value = chip_sum(direction * (hops + 1 - t), half)
            if t > 1:
                last[n].wait_recv()
                value = value + landed[slot - 1]
            sums[slot] = value
            copy = remote(
                sums.at[slot], landed.at[slot], chain_send.at[slot], chain_recv.at[slot], side[direction]
            )
            copy.start()
            last[n] = copy
            sends.append(copy)

    gathers = []
    first = {}
    for half, (a, b) in ((1, (2, 1)), (0, (3, 0))):
        value = chip_sum(0, half)
        for n in (a, b):
            last[n].wait_recv()
            value = value + landed[n * 4 + CHAINS[n][2] - 1]
        own_buf[pl.ds(half * HALF, HALF), :] = value.astype(jnp.bfloat16)
        at = rows_at(row * SHARD + half * HALF, HALF, HALF)
        out_ref[at, :] = value.astype(jnp.bfloat16)
        src = own_buf.at[pl.ds(half * HALF, HALF), :]
        for n, (direction, h, hops) in enumerate(CHAINS):
            if h == half:
                copy = remote(
                    src, out_ref.at[at, :], gather_send.at[n * 4], gather_recv.at[n * 4], side[direction]
                )
                copy.start()
                first[n] = copy
                sends.append(copy)
        copy = remote(src, out_ref.at[at, :], twin_send.at[half], twin_recv.at[half], twin)
        copy.start()
        gathers.append(copy)
        sends.append(copy)
    for t in range(1, 5):
        for n in (1, 2, 0, 3):
            direction, half, hops = CHAINS[n]
            if t > hops:
                continue
            first[n].wait_recv()
            at = rows_at((2 * ring(-direction * t) + core) * SHARD + half * HALF, HALF, HALF)
            if t < hops:
                copy = remote(
                    out_ref.at[at, :], out_ref.at[at, :],
                    gather_send.at[n * 4 + t], gather_recv.at[n * 4 + t], side[direction],
                )
                copy.start()
                first[n] = copy
                sends.append(copy)
            slot = 2 + n * 4 + t - 1
            copy = remote(out_ref.at[at, :], out_ref.at[at, :], twin_send.at[slot], twin_recv.at[slot], twin)
            copy.start()
            gathers.append(copy)
            sends.append(copy)
    for copy in gathers:
        copy.wait_recv()
    for copy in sends:
        copy.wait_send()
    for item in seen:
        pair[item].wait_send()


def exchange_columns(partial):
    dma = pltpu.SemaphoreType.DMA
    return pl.pallas_call(
        column_exchange,
        out_shape=jax.ShapeDtypeStruct((FULL, K), jnp.bfloat16),
        in_specs=[whole()],
        out_specs=whole(),
        scratch_shapes=[
            vmem((16, HALF, K), jnp.float32),
            vmem((16, HALF, K), jnp.float32),
            vmem((16, HALF, K), jnp.float32),
            dma((16,)),
            dma((16,)),
            dma((16,)),
            dma((16,)),
            vmem((SHARD, K), jnp.bfloat16),
            dma((16,)),
            dma((16,)),
            dma((18,)),
            dma((18,)),
        ],
        compiler_params=pltpu.CompilerParams(
            collective_id=1, has_side_effects=True, vmem_limit_bytes=VMEM_LIMIT
        ),
        name="exchange_columns",
    )(partial)


RS_STREAMS = 8
RS_Q = SHARD // RS_STREAMS


def row_reduce(
    part_ref, ns_ref, gram_ref, land0, land1, land2, land3, acc, s0, r0, s1, r1,
    local, cols_in, col_send, col_recv, half_out, half_in, half_send, half_recv,
    z_in, z_send, z_recv, slab, out_send, out_recv,
):
    row, me = lax.axis_index("row"), lax.axis_index("col")
    z, core = lax.div(row, 2), lax.rem(row, 2)
    other = row + 1 - 2 * core
    twin = (other, me)
    near = [(row, flip(me, g)) for g in range(4)]
    plane = [lax.rem(me + d, 16) for d in range(1, 16)]
    column = [2 * lax.rem(z + d, 8) + core for d in range(1, 8)]
    greet(
        [(row, p) for p in plane] + [(other, p) for p in plane] + [twin] + [(q, me) for q in column]
    )
    sends = []

    combos = [(a, b, c) for a in (0, 1) for b in (0, 1) for c in (0, 1)]
    waits = {}

    def moved(k, combo):
        block = me
        for bit, i in zip(combo, (1, 2, 3)):
            if bit:
                block = flip(block, (k + i) % 4)
        return block

    for k in range(RS_STREAMS):
        copies = []
        for n, combo in enumerate(combos):
            block = flip(moved(k, combo), k % 4)
            at = rows_at(block * SHARD + k * RS_Q, RS_Q, 16)
            slot = k * 8 + n
            copy = remote(part_ref.at[at, :], land0.at[slot], s0.at[slot], r0.at[slot], near[k % 4])
            copy.start()
            copies.append(copy)
        waits[k] = copies
        sends += copies
    lands = {1: land1, 2: land2, 3: land3}
    for step in range(1, 5):
        for k in range(RS_STREAMS):
            size = 2 ** (4 - step)
            for copy in waits[k]:
                copy.wait_recv()
            if step == 1:
                for n in range(size - 1, -1, -1):
                    at = rows_at(moved(k, combos[n]) * SHARD + k * RS_Q, RS_Q, 16)
                    slot = k * 8 + n
                    acc[slot] = part_ref[at, :].astype(jnp.float32) + land0[slot].astype(jnp.float32)
            else:
                land = lands[step - 1]
                for n in range(size):
                    acc[k * 8 + n] = acc[k * 8 + n] + land[k * size + n].astype(jnp.float32)
            if step < 4:
                half = size // 2
                slot = k * 3 + step - 1
                copy = remote(
                    acc.at[pl.ds(k * 8 + half, half)],
                    lands[step].at[pl.ds(k * half, half)],
                    s1.at[slot],
                    r1.at[slot],
                    near[(k + step) % 4],
                )
                copy.start()
                waits[k] = [copy]
                sends.append(copy)
            else:
                ns_ref[pl.ds(k * RS_Q, RS_Q), :] = acc[k * 8]

    rows = ns_ref[...]
    local[...] = lax.dot_general(
        rows, rows, (((0,), (0,)), ((), ())), precision=HI, preferred_element_type=jnp.float32
    )
    copies = []
    for d, p in enumerate(plane):
        copy = remote(
            local.at[rows_at(p * 16, 16, 16), :], cols_in.at[d], col_send.at[d], col_recv.at[d], (row, p)
        )
        copy.start()
        copies.append(copy)
    sends += copies
    total = local[rows_at(me * 16, 16, 16), :]
    for d, copy in enumerate(copies):
        copy.wait_recv()
        total = total + cols_in[d]
    half_out[...] = total
    copy = remote(half_out.at[rows_at((1 - core) * 8, 8, 8), :], half_in, half_send, half_recv, twin)
    copy.start()
    copy.wait_recv()
    sends.append(copy)
    slab[...] = half_out[rows_at(core * 8, 8, 8), :] + half_in[...]
    copies = []
    for d, q in enumerate(column):
        copy = remote(slab, z_in.at[z], z_send.at[d], z_recv.at[d], (q, me))
        copy.start()
        copies.append(copy)
    sends += copies
    z_in[z] = slab[...]
    for copy in copies:
        copy.wait_recv()
    total = z_in[0]
    for d in range(1, 8):
        total = total + z_in[d]
    at = rows_at(me * 16 + core * 8, 8, 8)
    gram_ref[at, :] = total * (1.0 / ROWS)
    copies = []
    for n, device in enumerate([twin] + [(r, p) for p in plane for r in (row, other)]):
        copy = remote(gram_ref.at[at, :], gram_ref.at[at, :], out_send.at[n], out_recv.at[n], device)
        copy.start()
        copies.append(copy)
    for copy in copies:
        copy.wait_recv()
    for copy in sends + copies:
        copy.wait_send()


def reduce_rows(partial):
    dma = pltpu.SemaphoreType.DMA
    f32 = jnp.float32
    n = RS_STREAMS
    return pl.pallas_call(
        row_reduce,
        out_shape=(
            jax.ShapeDtypeStruct((SHARD, K), f32),
            jax.ShapeDtypeStruct((K, K), f32),
        ),
        in_specs=[whole()],
        out_specs=(whole(), whole()),
        scratch_shapes=[
            vmem((n * 8, RS_Q, K), partial.dtype),
            vmem((n * 4, RS_Q, K), f32),
            vmem((n * 2, RS_Q, K), f32),
            vmem((n, RS_Q, K), f32),
            vmem((n * 8, RS_Q, K), f32),
            dma((n * 8,)),
            dma((n * 8,)),
            dma((n * 3,)),
            dma((n * 3,)),
            vmem((K, K), f32),
            vmem((15, 16, K), f32),
            dma((15,)),
            dma((15,)),
            vmem((16, K), f32),
            vmem((8, K), f32),
            dma,
            dma,
            vmem((8, 8, K), f32),
            dma((7,)),
            dma((7,)),
            vmem((8, K), f32),
            dma((31,)),
            dma((31,)),
        ],
        compiler_params=pltpu.CompilerParams(
            collective_id=2, has_side_effects=True, vmem_limit_bytes=VMEM_LIMIT
        ),
        name="reduce_rows",
    )(partial)


OUTER = 64


def factor_kernel(gram_ref, ns_ref, basis_ref, factor_ref, work):
    i0 = lax.broadcasted_iota(jnp.int32, (K, K), 0)
    i1 = lax.broadcasted_iota(jnp.int32, (K, K), 1)
    work[:, :K] = gram_ref[...]
    work[:, K:] = (i0 == i1).astype(jnp.float32)
    sub = lax.broadcasted_iota(jnp.int32, (8, 128), 0)
    for o in range(K // OUTER):
        base = o * OUTER
        for p in range(OUTER // 8):
            j = base + p * 8
            panel = work[pl.ds(j, 8), :]
            if p:
                done = work[pl.ds(base, p * 8), :]
                panel = panel - lax.dot_general(
                    done[:, j : j + 8], done, (((0,), (0,)), ((), ())),
                    precision=HI, preferred_element_type=jnp.float32,
                )
            parts = [panel[:, q * 128 : (q + 1) * 128] for q in range(4)]
            cols = [jnp.broadcast_to(panel[:, j + k : j + k + 1], (8, 128)) for k in range(8)]
            for i in range(8):
                scale = lax.rsqrt(jnp.broadcast_to(cols[i][i : i + 1, :], (8, 128)))
                down = jnp.where(sub > i, cols[i] * scale, 0.0)
                for k in range(i + 1, 8):
                    cols[k] = cols[k] - down * (jnp.broadcast_to(cols[k][i : i + 1, :], (8, 128)) * scale)
                for q in range(4):
                    line = jnp.broadcast_to(parts[q][i : i + 1, :], (8, 128)) * scale
                    parts[q] = jnp.where(sub == i, line, parts[q] - down * line)
            for q in range(4):
                work[pl.ds(j, 8), q * 128 : (q + 1) * 128] = parts[q]
        rest = K - base - OUTER
        if rest:
            done = work[pl.ds(base, OUTER), :]
            work[pl.ds(base + OUTER, rest), :] = work[pl.ds(base + OUTER, rest), :] - lax.dot_general(
                done[:, base + OUTER : K], done, (((0,), (0,)), ((), ())),
                precision=HI, preferred_element_type=jnp.float32,
            )
    factor_ref[...] = jnp.where(i1 >= i0, work[:, :K], 0.0)
    inverse_t = jnp.where(i0 >= i1, work[:, K:], 0.0)
    basis_ref[...] = lax.dot_general(
        ns_ref[...], inverse_t, (((1,), (1,)), ((), ())), precision=HI, preferred_element_type=jnp.float32
    )


def factor_and_basis(gram, ns):
    return pl.pallas_call(
        factor_kernel,
        out_shape=(
            jax.ShapeDtypeStruct((SHARD, K), jnp.float32),
            jax.ShapeDtypeStruct((K, K), jnp.float32),
        ),
        in_specs=[whole(), whole()],
        out_specs=(whole(), whole()),
        scratch_shapes=[vmem((K, 2 * K), jnp.float32)],
        compiler_params=pltpu.CompilerParams(vmem_limit_bytes=VMEM_LIMIT),
        name="factor",
    )(gram, ns)


def body(tiles, tile_rows, tile_cols, tile_counts, sketch):
    local_tiles = tiles[0, 0]
    rows, cols, count = tile_rows[0, 0], tile_cols[0, 0], tile_counts[0]
    gathered = gather_sketch(sketch)
    partial_cols = multiply(True, jnp.float32, local_tiles, rows, cols, count, gathered)
    columns = exchange_columns(partial_cols)
    partial_rows = multiply(False, jnp.bfloat16, local_tiles, rows, cols, count, columns)
    ns, gram = reduce_rows(partial_rows)
    return factor_and_basis(gram, ns)


def solution(mesh):
    return jax.shard_map(
        body,
        mesh=mesh,
        in_specs=(
            P("row", "col", None, None, None),
            P("row", "col", None),
            P("row", "col", None),
            P("row", "col"),
            P(("row", "col"), None),
        ),
        out_specs=(P(("row", "col"), None), P()),
        check_vma=False,
    )
```

```python
import functools
import heapq

import jax
import jax.numpy as jnp
from jax import lax
from jax.experimental import pallas as pl
from jax.experimental.pallas import tpu as pltpu
from jax.sharding import PartitionSpec as P

TILE = 512
K = 256
H = 128
BR = 12
BC = 12
CAP = 16
SHARD = 384
HALF = SHARD // 2
FULL = 6144
UNIT = 32
TU = TILE // UNIT
HU = 192 // UNIT
ROWS = 98304
STREAMS = 4
Q = SHARD // STREAMS
MESH = pl.DeviceIdType.MESH
HI = lax.Precision.HIGHEST
VMEM_LIMIT = 60 * 1024 * 1024
F32 = jnp.float32
BF16 = jnp.bfloat16
CHAINS = ((1, 0, 4), (-1, 1, 4), (1, 1, 3), (-1, 0, 3))
WIRE = (BF16, F32, F32, F32)


def vmem(shape, dtype):
    return pltpu.VMEM(shape, dtype)


def dma(n):
    return pltpu.SemaphoreType.DMA((n,))


def whole():
    return pl.BlockSpec(memory_space=pltpu.VMEM)


def flip(i, g):
    x, y = lax.rem(i, 4), lax.div(i, 4)
    if g == 0:
        return i + 1 - 2 * lax.rem(x, 2)
    if g == 1:
        return i + 3 - 2 * x
    if g == 2:
        return i + 4 - 8 * lax.rem(y, 2)
    return i + 12 - 8 * y


def rows_at(start, size, step):
    return pl.ds(pl.multiple_of(start, step), size)


def remote(src, dst, send_sem, recv_sem, device):
    return pltpu.make_async_remote_copy(
        src_ref=src,
        dst_ref=dst,
        send_sem=send_sem,
        recv_sem=recv_sem,
        device_id=device,
        device_id_type=MESH,
    )


def last_step(mask):
    return mask.bit_length() - 1


def first_step(mask):
    return (mask & -mask).bit_length() - 1


def interleave(processes):
    queue = []
    for n, process in enumerate(processes):
        heapq.heappush(queue, (next(process), n, process))
    while queue:
        _, n, process = heapq.heappop(queue)
        try:
            heapq.heappush(queue, (next(process), n, process))
        except StopIteration:
            pass


HALF_SCRATCH = dict(
    shard=lambda: vmem((SHARD // UNIT, UNIT, H), BF16),
    gathered=lambda: vmem((FULL // UNIT, UNIT, H), BF16),
    ag_send=lambda: dma(STREAMS * 15),
    ag_recv=lambda: dma(STREAMS * 15),
    acc=lambda: vmem((CAP + 1, TILE, H), F32),
    part=lambda: vmem((FULL, H), F32),
    pair_buf=lambda: vmem((16, HALF, H), F32),
    sums=lambda: vmem((16, HALF, H), F32),
    landed=lambda: vmem((16, HALF, H), F32),
    pair_send=lambda: dma(16),
    pair_recv=lambda: dma(16),
    chain_send=lambda: dma(16),
    chain_recv=lambda: dma(16),
    own=lambda: vmem((SHARD // UNIT, UNIT, H), BF16),
    columns=lambda: vmem((FULL // UNIT, UNIT, H), BF16),
    gather_send=lambda: dma(16),
    gather_recv=lambda: dma(16),
    twin_send=lambda: dma(18),
    twin_recv=lambda: dma(18),
    part2=lambda: vmem((FULL, H), BF16),
    land0=lambda: vmem((STREAMS * 8, Q, H), BF16),
    land1=lambda: vmem((STREAMS * 4, Q, H), WIRE[1]),
    land2=lambda: vmem((STREAMS * 3, Q, H), F32),
    acc2=lambda: vmem((STREAMS * 8, Q, H), F32),
    wire1=lambda: vmem((STREAMS * 4, Q, H), BF16),
    rs_send=lambda: dma(STREAMS * 15),
    rs_recv=lambda: dma(STREAMS * 15),
)

SHARED_SCRATCH = dict(
    tiles=lambda: vmem((CAP, TILE, TILE), BF16),
    tile_sem=lambda: dma(CAP),
    gram_part=lambda: vmem((K, K), F32),
    slabs=lambda: vmem((31, 8, K), F32),
    slab=lambda: vmem((8, K), F32),
    slab_send=lambda: dma(31),
    slab_recv=lambda: dma(31),
    z_in=lambda: vmem((8, 8, K), F32),
    z_send=lambda: dma(7),
    z_recv=lambda: dma(7),
    out_send=lambda: dma(31),
    out_recv=lambda: dma(31),
)


class Refs:
    pass


def named(names, refs):
    out = Refs()
    for name, ref in zip(names, refs):
        setattr(out, name, ref)
    return out


def iterate(plan_ref, tiles_ref, sketch_ref, ns_ref, gram_ref, *scratch):
    nh = len(HALF_SCRATCH)
    halves = [named(HALF_SCRATCH, scratch[i * nh : (i + 1) * nh]) for i in (0, 1)]
    shared = named(SHARED_SCRATCH, scratch[2 * nh :])

    row, me = lax.axis_index("row"), lax.axis_index("col")
    z, core = lax.div(row, 2), lax.rem(row, 2)
    other = row + 1 - 2 * core
    twin = (other, me)
    near = [(row, flip(me, g)) for g in range(4)]
    plane = [lax.rem(me + d, 16) for d in range(1, 16)]

    def ring(d):
        return lax.rem(z + d + 8, 8)

    side = {1: (2 * ring(1) + core, me), -1: (2 * ring(-1) + core, me)}
    column = [(2 * ring(d) + core, me) for d in range(1, 8)]
    everyone = [twin] + [(r, p) for p in plane for r in (row, other)]

    loads = []
    for s in range(CAP):
        load = pltpu.make_async_copy(tiles_ref.at[s], shared.tiles.at[s], shared.tile_sem.at[s])
        load.start()
        loads.append(load)
    for i, half in enumerate(halves):
        half.shard[...] = sketch_ref[:, i * H : (i + 1) * H].reshape(SHARD // UNIT, UNIT, H)

    barrier = pltpu.get_barrier_semaphore()
    for device in everyone + column:
        pl.semaphore_signal(barrier, inc=1, device_id=device, device_id_type=MESH)
    pl.semaphore_wait(barrier, len(everyone) + len(column))

    sends = []

    def gather(half, start, flow):
        copies = {}
        half.gathered[pl.ds(me * (SHARD // UNIT), SHARD // UNIT)] = half.shard[...]

        def block_at(k, mask):
            block = me
            for s in range(4):
                if mask >> s & 1:
                    block = flip(block, (k + s) % 4)
            return pl.ds(block * (SHARD // UNIT) + k * (Q // UNIT), Q // UNIT)

        def forward(k, mask, s):
            at = block_at(k, mask)
            src = half.shard.at[pl.ds(k * (Q // UNIT), Q // UNIT)] if mask == 0 else half.gathered.at[at]
            slot = k * 15 + (mask | 1 << s) - 1
            copy = remote(
                src, half.gathered.at[at], half.ag_send.at[slot], half.ag_recv.at[slot], near[(k + s) % 4]
            )
            copy.start()
            copies[k, mask | 1 << s] = copy
            sends.append(copy)

        for s in range(4):
            for k in range(STREAMS):
                forward(k, 0, s)
        masks = sorted(range(1, 16), key=lambda m: (m.bit_count(), last_step(m), m))
        n = 0
        for mask in masks:
            for k in range(STREAMS):
                yield start + 2 + flow * n / 60
                n += 1
                copies[k, mask].wait_recv()
                for s in range(last_step(mask) + 1, 4):
                    forward(k, mask, s)

    def multiply(half, transposed, source, result, start, per_tile):
        base = 0 if transposed else PLAN
        dims = (((0,), (0,)), ((), ())) if transposed else (((1,), (0,)), ((), ()))
        for s in range(CAP):
            yield start + per_tile * s
            if loads[s] is not None:
                loads[s].wait()
                loads[s] = None
            block = source[pl.ds(plan_ref[base + s] * TU, TU)].reshape(TILE, H)
            for u in range(2):
                part = pl.ds(u * 256, 256)
                tile = shared.tiles[s, :, part] if transposed else shared.tiles[s, part, :]
                half.acc[s + 1, part, :] = half.acc[plan_ref[base + CAP + s], part, :] + lax.dot_general(
                    tile, block, dims, preferred_element_type=F32
                )
        for b in range(BR):
            yield start + per_tile * CAP + 0.08 * b
            result[pl.ds(b * TILE, TILE), :] = half.acc[plan_ref[base + 2 * CAP + b]].astype(result.dtype)

    def exchange(half, start, ring_start, reduce_flow, gather_flow):
        yield start
        order = []
        for t in range(1, 5):
            for direction, part, hops in CHAINS:
                if t <= hops:
                    item = (direction * (hops + 1 - t) % 8, part)
                    if item not in order:
                        order.append(item)
        order += [(0, 0), (0, 1)]
        pair = {}
        for d, part in order:
            slot = d * 2 + part
            theirs = rows_at((2 * ring(d) + 1 - core) * SHARD + part * HALF, HALF, HALF)
            pair[d, part] = remote(
                half.part.at[theirs, :], half.pair_buf.at[slot],
                half.pair_send.at[slot], half.pair_recv.at[slot], twin,
            )
            pair[d, part].start()
            sends.append(pair[d, part])
        arrived = set()

        def chip_sum(d, part):
            d = d % 8
            slot = d * 2 + part
            if (d, part) not in arrived:
                pair[d, part].wait_recv()
                arrived.add((d, part))
            mine = rows_at((2 * ring(d) + core) * SHARD + part * HALF, HALF, HALF)
            return half.part[mine, :] + half.pair_buf[slot]

        last = {}
        n_sent = 0
        for t in range(1, 5):
            for n, (direction, part, hops) in enumerate(CHAINS):
                if t > hops:
                    continue
                yield ring_start + 2 + reduce_flow * n_sent / 14
                n_sent += 1
                slot = n * 4 + t - 1
                value = chip_sum(direction * (hops + 1 - t), part)
                if t > 1:
                    last[n].wait_recv()
                    value = value + half.landed[slot - 1]
                half.sums[slot] = value
                copy = remote(
                    half.sums.at[slot], half.landed.at[slot],
                    half.chain_send.at[slot], half.chain_recv.at[slot], side[direction],
                )
                copy.start()
                last[n] = copy
                sends.append(copy)
        begin = ring_start + 4 + reduce_flow
        twins = []
        moving = {}

        def spread(src, at, slot):
            copy = remote(src, half.columns.at[at], half.twin_send.at[slot], half.twin_recv.at[slot], twin)
            copy.start()
            twins.append(copy)
            sends.append(copy)

        def pass_on(src, at, n, t):
            slot = n * 4 + t
            copy = remote(
                src, half.columns.at[at],
                half.gather_send.at[slot], half.gather_recv.at[slot], side[CHAINS[n][0]],
            )
            copy.start()
            moving[n] = copy
            sends.append(copy)

        for part, (a, b) in ((1, (2, 1)), (0, (3, 0))):
            yield begin
            value = chip_sum(0, part)
            for n in (a, b):
                last[n].wait_recv()
                value = value + half.landed[n * 4 + CHAINS[n][2] - 1]
            local = pl.ds(part * HU, HU)
            rounded = value.astype(BF16).reshape(HU, UNIT, H)
            half.own[local] = rounded
            at = pl.ds((row * 2 + part) * HU, HU)
            half.columns[at] = rounded
            for n in range(4):
                if CHAINS[n][1] == part:
                    pass_on(half.own.at[local], at, n, 0)
            spread(half.own.at[local], at, part)
        n_got = 0
        for t in range(1, 5):
            for n in (1, 2, 0, 3):
                direction, part, hops = CHAINS[n]
                if t > hops:
                    continue
                yield begin + 2 + gather_flow * n_got / 14
                n_got += 1
                moving[n].wait_recv()
                at = pl.ds(((2 * ring(-direction * t) + core) * 2 + part) * HU, HU)
                if t < hops:
                    pass_on(half.columns.at[at], at, n, t)
                spread(half.columns.at[at], at, 2 + n * 4 + t - 1)
        for copy in twins:
            yield begin + 3 + gather_flow
            copy.wait_recv()

    def reduce(half, lane, start, flow):
        yield start
        copies = {}

        def block_at(k, mask):
            block = me
            for s in range(4):
                if mask >> s & 1:
                    block = flip(block, (k + s) % 4)
            return rows_at(block * SHARD + k * Q, Q, 16)

        def landing(k, s, mask):
            if s == 0:
                return half.land0.at[k * 8 + mask // 2]
            if s == 1:
                return half.land1.at[k * 4 + mask // 4]
            return half.land2.at[k * 3 + (mask // 8 if s == 2 else 2)]

        def send(k, mask):
            s = first_step(mask)
            if s == 0:
                src = half.part2.at[block_at(k, mask), :]
            elif WIRE[s] == BF16:
                half.wire1[k * 4 + mask // 4] = half.acc2[k * 8 + mask // 2].astype(BF16)
                src = half.wire1.at[k * 4 + mask // 4]
            else:
                src = half.acc2.at[k * 8 + mask // 2]
            slot = k * 15 + mask - 1
            copy = remote(
                src, landing(k, s, mask ^ (1 << s)), half.rs_send.at[slot], half.rs_recv.at[slot],
                near[(k + s) % 4],
            )
            copy.start()
            copies[k, mask] = copy
            sends.append(copy)

        def urgency(mask):
            rest = mask & ~1
            return (first_step(rest) if rest else 4, -mask)

        for mask in sorted((m for m in range(16) if m & 1), key=urgency):
            for k in range(STREAMS):
                send(k, mask)
        n = 0
        entries = sorted((m for m in range(16) if not m & 1), key=lambda m: (first_step(m) if m else 4, -m))
        for mask in entries:
            steps = first_step(mask) if mask else 4
            for k in range(STREAMS):
                yield start + 2.5 + flow * n / 32
                n += 1
                value = half.part2[block_at(k, mask), :].astype(F32)
                for s in range(steps):
                    copies[k, mask | 1 << s].wait_recv()
                    value = value + landing(k, s, mask)[...].astype(F32)
                if mask:
                    half.acc2[k * 8 + mask // 2] = value
                    send(k, mask)
                else:
                    ns_ref[pl.ds(k * Q, Q), pl.ds(lane, H)] = value

    def prepare():
        yield 0.5
        for half in halves:
            half.acc[0] = jnp.zeros((TILE, H), F32)

    a, b = halves

    def first():
        yield from gather(a, 0.0, 8.0)
        yield from multiply(a, True, a.gathered, a.part, 10.5, 0.35)
        yield from exchange(a, 17.5, 17.5, 14.8, 7.4)
        yield from multiply(a, False, a.columns, a.part2, 46.0, 0.35)
        yield from reduce(a, 0, 53.0, 12.0)

    def second():
        yield 7.0
        yield from gather(b, 7.0, 8.0)
        yield from multiply(b, True, b.gathered, b.part, 18.0, 0.35)
        yield from exchange(b, 25.0, 34.0, 20.0, 9.0)
        yield from multiply(b, False, b.columns, b.part2, 69.0, 0.35)
        yield from reduce(b, H, 76.0, 12.0)

    interleave([first(), prepare(), second()])

    rows = ns_ref[...]
    shared.gram_part[...] = lax.dot_general(
        rows, rows, (((0,), (0,)), ((), ())), precision=HI, preferred_element_type=F32
    )
    mine = rows_at(row * 0 + me * 16 + core * 8, 8, 8)
    copies = []
    for n, (r, p) in enumerate(everyone):
        theirs = rows_at(p * 16 + lax.rem(r, 2) * 8, 8, 8)
        copy = remote(
            shared.gram_part.at[theirs, :], shared.slabs.at[n], shared.slab_send.at[n], shared.slab_recv.at[n], (r, p)
        )
        copy.start()
        copies.append(copy)
    sends += copies
    total = shared.gram_part[mine, :]
    for n, copy in enumerate(copies):
        copy.wait_recv()
        total = total + shared.slabs[n]
    shared.slab[...] = total
    copies = []
    for d, device in enumerate(column):
        copy = remote(shared.slab, shared.z_in.at[z], shared.z_send.at[d], shared.z_recv.at[d], device)
        copy.start()
        copies.append(copy)
    sends += copies
    shared.z_in[z] = total
    for copy in copies:
        copy.wait_recv()
    total = shared.z_in[0]
    for d in range(1, 8):
        total = total + shared.z_in[d]
    gram_ref[mine, :] = total * (1.0 / ROWS)
    copies = []
    for n, device in enumerate(everyone):
        copy = remote(gram_ref.at[mine, :], gram_ref.at[mine, :], shared.out_send.at[n], shared.out_recv.at[n], device)
        copy.start()
        copies.append(copy)
    for copy in copies:
        copy.wait_recv()
    for copy in sends + copies:
        copy.wait_send()


PLAN = 2 * CAP + BR


def plan_kernel(rows_ref, cols_ref, count_ref, plan_ref):
    count = count_ref[0]
    for base, source, target in ((0, rows_ref, cols_ref), (PLAN, cols_ref, rows_ref)):
        to = [target[t] for t in range(CAP)]
        for s in range(CAP):
            at = jnp.int32(0)
            for t in range(s):
                at = jnp.where(to[t] == to[s], t + 1, at)
            plan_ref[base + s] = source[s]
            plan_ref[base + CAP + s] = at
        for b in range(BR):
            at = jnp.int32(0)
            for t in range(CAP):
                at = jnp.where((to[t] == b) & (t < count), t + 1, at)
            plan_ref[base + 2 * CAP + b] = at


def make_plan(rows, cols, count):
    smem = pl.BlockSpec(memory_space=pltpu.SMEM)
    return pl.pallas_call(
        plan_kernel,
        out_shape=jax.ShapeDtypeStruct((2 * PLAN,), jnp.int32),
        in_specs=[smem] * 3,
        out_specs=smem,
        name="plan",
    )(rows, cols, count)


def iterate_call(plan, tiles, sketch):
    smem = pl.BlockSpec(memory_space=pltpu.SMEM)
    scratch = [make() for _ in range(2) for make in HALF_SCRATCH.values()]
    scratch += [make() for make in SHARED_SCRATCH.values()]
    return pl.pallas_call(
        iterate,
        out_shape=(
            jax.ShapeDtypeStruct((SHARD, K), F32),
            jax.ShapeDtypeStruct((K, K), F32),
        ),
        in_specs=[smem, pl.BlockSpec(memory_space=pl.ANY), whole()],
        out_specs=(whole(), whole()),
        scratch_shapes=scratch,
        compiler_params=pltpu.CompilerParams(
            collective_id=0, has_side_effects=True, vmem_limit_bytes=VMEM_LIMIT
        ),
        name="iterate",
    )(plan, tiles, sketch)


OUTER = 64


def factor_kernel(gram_ref, ns_ref, basis_ref, factor_ref, work):
    i0 = lax.broadcasted_iota(jnp.int32, (K, K), 0)
    i1 = lax.broadcasted_iota(jnp.int32, (K, K), 1)
    work[:, :K] = gram_ref[...]
    work[:, K:] = (i0 == i1).astype(F32)
    sub = lax.broadcasted_iota(jnp.int32, (8, 128), 0)
    for o in range(K // OUTER):
        base = o * OUTER
        for p in range(OUTER // 8):
            j = base + p * 8
            panel = work[pl.ds(j, 8), :]
            if p:
                done = work[pl.ds(base, p * 8), :]
                panel = panel - lax.dot_general(
                    done[:, j : j + 8], done, (((0,), (0,)), ((), ())),
                    precision=HI, preferred_element_type=F32,
                )
            parts = [panel[:, q * 128 : (q + 1) * 128] for q in range(4)]
            cols = [jnp.broadcast_to(panel[:, j + k : j + k + 1], (8, 128)) for k in range(8)]
            for i in range(8):
                scale = lax.rsqrt(jnp.broadcast_to(cols[i][i : i + 1, :], (8, 128)))
                down = jnp.where(sub > i, cols[i] * scale, 0.0)
                for k in range(i + 1, 8):
                    cols[k] = cols[k] - down * (jnp.broadcast_to(cols[k][i : i + 1, :], (8, 128)) * scale)
                for q in range(4):
                    line = jnp.broadcast_to(parts[q][i : i + 1, :], (8, 128)) * scale
                    parts[q] = jnp.where(sub == i, line, parts[q] - down * line)
            for q in range(4):
                work[pl.ds(j, 8), q * 128 : (q + 1) * 128] = parts[q]
        rest = K - base - OUTER
        if rest:
            done = work[pl.ds(base, OUTER), :]
            work[pl.ds(base + OUTER, rest), :] = work[pl.ds(base + OUTER, rest), :] - lax.dot_general(
                done[:, base + OUTER : K], done, (((0,), (0,)), ((), ())),
                precision=HI, preferred_element_type=F32,
            )
    factor_ref[...] = jnp.where(i1 >= i0, work[:, :K], 0.0)
    inverse_t = jnp.where(i0 >= i1, work[:, K:], 0.0)
    basis_ref[...] = lax.dot_general(
        ns_ref[...], inverse_t, (((1,), (1,)), ((), ())), precision=HI, preferred_element_type=F32
    )


def factor_and_basis(gram, ns):
    return pl.pallas_call(
        factor_kernel,
        out_shape=(
            jax.ShapeDtypeStruct((SHARD, K), F32),
            jax.ShapeDtypeStruct((K, K), F32),
        ),
        in_specs=[whole(), whole()],
        out_specs=(whole(), whole()),
        scratch_shapes=[vmem((K, 2 * K), F32)],
        compiler_params=pltpu.CompilerParams(vmem_limit_bytes=VMEM_LIMIT),
        name="factor",
    )(gram, ns)


def body(tiles, tile_rows, tile_cols, tile_counts, sketch):
    plan = make_plan(tile_rows[0, 0], tile_cols[0, 0], tile_counts[0])
    ns, gram = iterate_call(plan, tiles[0, 0], sketch)
    return factor_and_basis(gram, ns)


def solution(mesh):
    return jax.shard_map(
        body,
        mesh=mesh,
        in_specs=(
            P("row", "col", None, None, None),
            P("row", "col", None),
            P("row", "col", None),
            P("row", "col"),
            P(("row", "col"), None),
        ),
        out_specs=(P(("row", "col"), None), P()),
        check_vma=False,
    )
```

```python
import functools
import heapq

import jax
import jax.numpy as jnp
from jax import lax
from jax.experimental import pallas as pl
from jax.experimental.pallas import tpu as pltpu
from jax.sharding import PartitionSpec as P

TILE = 512
K = 256
H = 128
BR = 12
BC = 12
CAP = 16
SHARD = 384
FULL = 6144
UNIT = 32
TU = TILE // UNIT
PU = 96 // UNIT
ROWS = 98304
STREAMS = 4
Q = SHARD // STREAMS
MESH = pl.DeviceIdType.MESH
HI = lax.Precision.HIGHEST
VMEM_LIMIT = 60 * 1024 * 1024
F32 = jnp.float32
BF16 = jnp.bfloat16
PARTS = 4
PART = SHARD // PARTS
CHAINS = tuple((1 - 2 * (p % 2), p, 4) for p in range(PARTS)) + tuple((2 * (p % 2) - 1, p, 3) for p in range(PARTS))
WIRE = (BF16, BF16, F32, F32)


def vmem(shape, dtype):
    return pltpu.VMEM(shape, dtype)


def dma(n):
    return pltpu.SemaphoreType.DMA((n,))


def whole():
    return pl.BlockSpec(memory_space=pltpu.VMEM)


def flip(i, g):
    x, y = lax.rem(i, 4), lax.div(i, 4)
    if g == 0:
        return i + 1 - 2 * lax.rem(x, 2)
    if g == 1:
        return i + 3 - 2 * x
    if g == 2:
        return i + 4 - 8 * lax.rem(y, 2)
    return i + 12 - 8 * y


def rows_at(start, size, step):
    return pl.ds(pl.multiple_of(start, step), size)


def remote(src, dst, send_sem, recv_sem, device):
    return pltpu.make_async_remote_copy(
        src_ref=src,
        dst_ref=dst,
        send_sem=send_sem,
        recv_sem=recv_sem,
        device_id=device,
        device_id_type=MESH,
    )


def last_step(mask):
    return mask.bit_length() - 1


def first_step(mask):
    return (mask & -mask).bit_length() - 1


def interleave(processes):
    queue = []
    for n, process in enumerate(processes):
        heapq.heappush(queue, (next(process), n, process))
    while queue:
        _, n, process = heapq.heappop(queue)
        try:
            heapq.heappush(queue, (next(process), n, process))
        except StopIteration:
            pass


def wide(x):
    return jnp.broadcast_to(x, (8, H))


def matmul(a, b, contract):
    return lax.dot_general(a, b, (contract, ((), ())), precision=HI, preferred_element_type=F32)


def eliminate(work):
    sub = lax.broadcasted_iota(jnp.int32, (8, H), 0)
    panels = H // 8
    below = None
    for p in range(panels):
        j = p * 8
        parts = [work[pl.ds(j, 8), :H], work[pl.ds(j, 8), H:]] if below is None else below
        cols = [wide(parts[0][:, j + k : j + k + 1]) for k in range(8)]
        below = None
        if p + 1 < panels:
            m = j + 8
            rows = work[pl.ds(m, 8), :]
            if p:
                done = work[pl.ds(0, j), :]
                rows = rows - matmul(done[:, m : m + 8], done, ((0,), (0,)))
            below = [rows[:, :H], rows[:, H:]]
            under = [wide(below[0][:, j + k : j + k + 1]) for k in range(8)]
        for i in range(8):
            scale = lax.rsqrt(wide(cols[i][i : i + 1, :]))
            down = jnp.where(sub > i, cols[i] * scale, 0.0)
            if below is not None:
                drop = under[i] * scale
            for k in range(i + 1, 8):
                line = wide(cols[k][i : i + 1, :]) * scale
                cols[k] = cols[k] - down * line
                if below is not None:
                    under[k] = under[k] - drop * line
            for q in range(2):
                line = wide(parts[q][i : i + 1, :]) * scale
                parts[q] = jnp.where(sub == i, line, parts[q] - down * line)
                if below is not None:
                    below[q] = below[q] - drop * line
        for q in range(2):
            work[pl.ds(j, 8), q * H : (q + 1) * H] = parts[q]
        yield


HALF_SCRATCH = dict(
    shard=lambda: vmem((SHARD // UNIT, UNIT, H), BF16),
    gathered=lambda: vmem((FULL // UNIT, UNIT, H), BF16),
    ag_send=lambda: dma(STREAMS * 15),
    ag_recv=lambda: dma(STREAMS * 15),
    acc=lambda: vmem((CAP + 1, TILE, H), F32),
    part=lambda: vmem((FULL, H), F32),
    pair_buf=lambda: vmem((8 * PARTS, PART, H), F32),
    sums=lambda: vmem((8 * PARTS, PART, H), F32),
    landed=lambda: vmem((8 * PARTS, PART, H), F32),
    pair_send=lambda: dma(8 * PARTS),
    pair_recv=lambda: dma(8 * PARTS),
    chain_send=lambda: dma(8 * PARTS),
    chain_recv=lambda: dma(8 * PARTS),
    own=lambda: vmem((SHARD // UNIT, UNIT, H), BF16),
    columns=lambda: vmem((FULL // UNIT, UNIT, H), BF16),
    gather_send=lambda: dma(8 * PARTS),
    gather_recv=lambda: dma(8 * PARTS),
    twin_send=lambda: dma(9 * PARTS),
    twin_recv=lambda: dma(9 * PARTS),
    part2=lambda: vmem((FULL, H), BF16),
    land0=lambda: vmem((STREAMS * 8, Q, H), BF16),
    land1=lambda: vmem((STREAMS * 4, Q, H), WIRE[1]),
    land2=lambda: vmem((STREAMS * 3, Q, H), F32),
    acc2=lambda: vmem((STREAMS * 8, Q, H), F32),
    wire1=lambda: vmem((STREAMS * 4, Q, H), BF16),
    rs_send=lambda: dma(STREAMS * 15),
    rs_recv=lambda: dma(STREAMS * 15),
)

SHARED_SCRATCH = dict(
    tiles=lambda: vmem((CAP, TILE, TILE), BF16),
    tile_sem=lambda: dma(CAP),
    work=lambda: vmem((H, 2 * H), F32),
    early_part=lambda: vmem((H, H), F32),
    early_in=lambda: vmem((16, 8, H), F32),
    early_row=lambda: vmem((16, 8, H), F32),
    early_slab=lambda: vmem((8, H), F32),
    early_sum=lambda: vmem((8, H), F32),
    early_gram=lambda: vmem((H, H), F32),
    early_send=lambda: dma(45),
    early_recv=lambda: dma(45),
    late_part=lambda: vmem((K, H), F32),
    slabs=lambda: vmem((31, 8, H), F32),
    slab=lambda: vmem((8, H), F32),
    slab_send=lambda: dma(31),
    slab_recv=lambda: dma(31),
    z_in=lambda: vmem((8, 8, H), F32),
    z_send=lambda: dma(7),
    z_recv=lambda: dma(7),
    out_send=lambda: dma(31),
    out_recv=lambda: dma(31),
)


class Refs:
    pass


def named(names, refs):
    out = Refs()
    for name, ref in zip(names, refs):
        setattr(out, name, ref)
    return out


def iterate(rows_ref, cols_ref, count_ref, tiles_ref, sketch_ref, ns_ref, early_ref, late_ref, *scratch):
    nh = len(HALF_SCRATCH)
    halves = [named(HALF_SCRATCH, scratch[i * nh : (i + 1) * nh]) for i in (0, 1)]
    shared = named(SHARED_SCRATCH, scratch[2 * nh :])

    row, me = lax.axis_index("row"), lax.axis_index("col")
    z, core = lax.div(row, 2), lax.rem(row, 2)
    other = row + 1 - 2 * core
    twin = (other, me)
    near = [(row, flip(me, g)) for g in range(4)]
    plane = [lax.rem(me + d, 16) for d in range(1, 16)]

    def ring(d):
        return lax.rem(z + d + 8, 8)

    side = {1: (2 * ring(1) + core, me), -1: (2 * ring(-1) + core, me)}
    column = [(2 * ring(d) + core, me) for d in range(1, 8)]
    everyone = [twin] + [(r, p) for p in plane for r in (row, other)]
    line = [(lax.rem(row + d, 16), me) for d in range(1, 16)]

    loads = []
    for s in range(CAP):
        load = pltpu.make_async_copy(tiles_ref.at[s], shared.tiles.at[s], shared.tile_sem.at[s])
        load.start()
        loads.append(load)
    for i, half in enumerate(halves):
        half.shard[...] = sketch_ref[:, i * H : (i + 1) * H].reshape(SHARD // UNIT, UNIT, H)

    barrier = pltpu.get_barrier_semaphore()
    greeted = everyone[1:] + line
    for device in greeted:
        pl.semaphore_signal(barrier, inc=1, device_id=device, device_id_type=MESH)
    pl.semaphore_wait(barrier, len(greeted))

    sends = []
    plan = {}

    def places(targets):
        to = [targets[t] for t in range(CAP)]
        count = count_ref[0]
        before, ends = [], []
        for s in range(CAP):
            at = jnp.int32(0)
            for t in range(s):
                at = jnp.where(to[t] == to[s], t + 1, at)
            before.append(at)
        for b in range(BR):
            at = jnp.int32(0)
            for t in range(CAP):
                at = jnp.where((to[t] == b) & (t < count), t + 1, at)
            ends.append(at)
        return before, ends

    def gather(half, start, flow):
        copies = {}
        half.gathered[pl.ds(me * (SHARD // UNIT), SHARD // UNIT)] = half.shard[...]

        def block_at(k, mask):
            block = me
            for s in range(4):
                if mask >> s & 1:
                    block = flip(block, (k + s) % 4)
            return pl.ds(block * (SHARD // UNIT) + k * (Q // UNIT), Q // UNIT)

        def forward(k, mask, s):
            at = block_at(k, mask)
            src = half.shard.at[pl.ds(k * (Q // UNIT), Q // UNIT)] if mask == 0 else half.gathered.at[at]
            slot = k * 15 + (mask | 1 << s) - 1
            copy = remote(
                src, half.gathered.at[at], half.ag_send.at[slot], half.ag_recv.at[slot], near[(k + s) % 4]
            )
            copy.start()
            copies[k, mask | 1 << s] = copy
            sends.append(copy)

        for s in range(4):
            for k in range(STREAMS):
                forward(k, 0, s)
        masks = sorted(range(1, 16), key=lambda m: (m.bit_count(), last_step(m), m))
        n = 0
        for mask in masks:
            for k in range(STREAMS):
                yield start + 3 + flow * n / 60
                n += 1
                copies[k, mask].wait_recv()
                for s in range(last_step(mask) + 1, 4):
                    forward(k, mask, s)

    def multiply(half, transposed, source, result, start, per_tile):
        src = rows_ref if transposed else cols_ref
        before, ends = plan[transposed]
        dims = (((0,), (0,)), ((), ())) if transposed else (((1,), (0,)), ((), ()))
        for s in range(CAP):
            yield start + per_tile * s
            if loads[s] is not None:
                loads[s].wait()
                loads[s] = None
            block = source[pl.ds(src[s] * TU, TU)].reshape(TILE, H)
            for u in range(2):
                part = pl.ds(u * 256, 256)
                tile = shared.tiles[s, :, part] if transposed else shared.tiles[s, part, :]
                half.acc[s + 1, part, :] = half.acc[before[s], part, :] + lax.dot_general(
                    tile, block, dims, preferred_element_type=F32
                )
        for b in range(BR):
            yield start + per_tile * CAP + 0.08 * b
            result[pl.ds(b * TILE, TILE), :] = half.acc[ends[b]].astype(result.dtype)

    def exchange(half, start, ring_start, reduce_flow, gather_flow):
        yield start
        order = []
        for t in range(1, 5):
            for direction, part, hops in CHAINS:
                if t <= hops:
                    item = (direction * (hops + 1 - t) % 8, part)
                    if item not in order:
                        order.append(item)
        order += [(0, part) for part in range(PARTS)]
        pair = {}
        for d, part in order:
            slot = d * PARTS + part
            theirs = rows_at((2 * ring(d) + 1 - core) * SHARD + part * PART, PART, PART)
            pair[d, part] = remote(
                half.part.at[theirs, :], half.pair_buf.at[slot],
                half.pair_send.at[slot], half.pair_recv.at[slot], twin,
            )
            pair[d, part].start()
            sends.append(pair[d, part])
        arrived = set()

        def chip_sum(d, part):
            d = d % 8
            slot = d * PARTS + part
            if (d, part) not in arrived:
                pair[d, part].wait_recv()
                arrived.add((d, part))
            mine = rows_at((2 * ring(d) + core) * SHARD + part * PART, PART, PART)
            return half.part[mine, :] + half.pair_buf[slot]

        last = {}
        n_sent = 0
        for t in range(1, 5):
            for n, (direction, part, hops) in enumerate(CHAINS):
                if t > hops:
                    continue
                yield ring_start + 2 + reduce_flow * n_sent / (7 * PARTS)
                n_sent += 1
                slot = n * 4 + t - 1
                value = chip_sum(direction * (hops + 1 - t), part)
                if t > 1:
                    last[n].wait_recv()
                    value = value + half.landed[slot - 1]
                half.sums[slot] = value
                copy = remote(
                    half.sums.at[slot], half.landed.at[slot],
                    half.chain_send.at[slot], half.chain_recv.at[slot], side[direction],
                )
                copy.start()
                last[n] = copy
                sends.append(copy)
        begin = ring_start + 3 + reduce_flow
        twins = []
        moving = {}

        def spread(src, at, slot):
            copy = remote(src, half.columns.at[at], half.twin_send.at[slot], half.twin_recv.at[slot], twin)
            copy.start()
            twins.append(copy)
            sends.append(copy)

        def pass_on(src, at, n, t):
            slot = n * 4 + t
            copy = remote(
                src, half.columns.at[at],
                half.gather_send.at[slot], half.gather_recv.at[slot], side[CHAINS[n][0]],
            )
            copy.start()
            moving[n] = copy
            sends.append(copy)

        for part in range(PARTS):
            yield begin + 0.1 * part
            value = chip_sum(0, part)
            for n in (part + PARTS, part):
                last[n].wait_recv()
                value = value + half.landed[n * 4 + CHAINS[n][2] - 1]
            local = pl.ds(part * PU, PU)
            rounded = value.astype(BF16).reshape(PU, UNIT, H)
            half.own[local] = rounded
            at = pl.ds((row * PARTS + part) * PU, PU)
            half.columns[at] = rounded
            for n in range(2 * PARTS):
                if CHAINS[n][1] == part:
                    pass_on(half.own.at[local], at, n, 0)
            spread(half.own.at[local], at, part)
        n_got = 0
        for t in range(1, 5):
            for n, (direction, part, hops) in enumerate(CHAINS):
                if t > hops:
                    continue
                yield begin + 2 + gather_flow * n_got / (7 * PARTS)
                n_got += 1
                moving[n].wait_recv()
                at = pl.ds(((2 * ring(-direction * t) + core) * PARTS + part) * PU, PU)
                if t < hops:
                    pass_on(half.columns.at[at], at, n, t)
                spread(half.columns.at[at], at, PARTS + n * 4 + t - 1)
        for copy in twins:
            yield begin + 3 + gather_flow
            copy.wait_recv()

    def reduce(half, lane, start, flow):
        yield start
        copies = {}

        def block_at(k, mask):
            block = me
            for s in range(4):
                if mask >> s & 1:
                    block = flip(block, (k + s) % 4)
            return rows_at(block * SHARD + k * Q, Q, 16)

        def landing(k, s, mask):
            if s == 0:
                return half.land0.at[k * 8 + mask // 2]
            if s == 1:
                return half.land1.at[k * 4 + mask // 4]
            return half.land2.at[k * 3 + (mask // 8 if s == 2 else 2)]

        def send(k, mask):
            s = first_step(mask)
            if s == 0:
                src = half.part2.at[block_at(k, mask), :]
            elif WIRE[s] == BF16:
                half.wire1[k * 4 + mask // 4] = half.acc2[k * 8 + mask // 2].astype(BF16)
                src = half.wire1.at[k * 4 + mask // 4]
            else:
                src = half.acc2.at[k * 8 + mask // 2]
            slot = k * 15 + mask - 1
            copy = remote(
                src, landing(k, s, mask ^ (1 << s)), half.rs_send.at[slot], half.rs_recv.at[slot],
                near[(k + s) % 4],
            )
            copy.start()
            copies[k, mask] = copy
            sends.append(copy)

        def urgency(mask):
            rest = mask & ~1
            return (first_step(rest) if rest else 4, -mask)

        for mask in sorted((m for m in range(16) if m & 1), key=urgency):
            for k in range(STREAMS):
                send(k, mask)
        n = 0
        entries = sorted((m for m in range(16) if not m & 1), key=lambda m: (first_step(m) if m else 4, -m))
        for mask in entries:
            steps = first_step(mask) if mask else 4
            for k in range(STREAMS):
                yield start + 2.5 + flow * n / 32
                n += 1
                value = half.part2[block_at(k, mask), :].astype(F32)
                for s in range(steps):
                    copies[k, mask | 1 << s].wait_recv()
                    value = value + landing(k, s, mask)[...].astype(F32)
                if mask:
                    half.acc2[k * 8 + mask // 2] = value
                    send(k, mask)
                else:
                    ns_ref[pl.ds(k * Q, Q), pl.ds(lane, H)] = value

    def prepare():
        yield 0.5
        for half in halves:
            half.acc[0] = jnp.zeros((TILE, H), F32)
        plan[True] = places(cols_ref)
        plan[False] = places(rows_ref)

    def early(start, plane_at, line_at, eliminate_at):
        yield start
        rows = ns_ref[:, :H]
        shared.early_part[...] = lax.dot_general(
            rows, rows, (((0,), (0,)), ((), ())), precision=HI, preferred_element_type=F32
        )
        mine = rows_at(me * 8, 8, 8)
        copies = []
        for d, p in enumerate(plane):
            copy = remote(
                shared.early_part.at[rows_at(p * 8, 8, 8), :], shared.early_in.at[d],
                shared.early_send.at[d], shared.early_recv.at[d], (row, p),
            )
            copy.start()
            copies.append(copy)
        sends.extend(copies)
        yield plane_at
        total = shared.early_part[mine, :]
        for d, copy in enumerate(copies):
            copy.wait_recv()
            total = total + shared.early_in[d]
        shared.early_slab[...] = total
        shared.early_row[row] = total
        copies = []
        for d, device in enumerate(line):
            copy = remote(
                shared.early_slab, shared.early_row.at[row],
                shared.early_send.at[15 + d], shared.early_recv.at[15 + d], device,
            )
            copy.start()
            copies.append(copy)
        sends.extend(copies)
        yield line_at
        for copy in copies:
            copy.wait_recv()
        total = shared.early_row[0]
        for d in range(1, 16):
            total = total + shared.early_row[d]
        total = total * (1.0 / ROWS)
        shared.early_sum[...] = total
        shared.early_gram[mine, :] = total
        copies = []
        for d, p in enumerate(plane):
            copy = remote(
                shared.early_sum, shared.early_gram.at[mine, :],
                shared.early_send.at[30 + d], shared.early_recv.at[30 + d], (row, p),
            )
            copy.start()
            copies.append(copy)
        sends.extend(copies)
        yield eliminate_at
        for copy in copies:
            copy.wait_recv()
        i0 = lax.broadcasted_iota(jnp.int32, (H, H), 0)
        i1 = lax.broadcasted_iota(jnp.int32, (H, H), 1)
        shared.work[:, :H] = shared.early_gram[...]
        shared.work[:, H:] = (i0 == i1).astype(F32)
        for n, _ in enumerate(eliminate(shared.work)):
            yield eliminate_at + 0.4 * n
        early_ref[:, :H] = jnp.where(i1 >= i0, shared.work[:, :H], 0.0)
        early_ref[:, H:] = jnp.where(i0 >= i1, shared.work[:, H:], 0.0)

    def late(start):
        yield start
        shared.late_part[...] = lax.dot_general(
            ns_ref[...], ns_ref[:, H:], (((0,), (0,)), ((), ())), precision=HI, preferred_element_type=F32
        )
        mine = rows_at(me * 16 + core * 8, 8, 8)
        copies = []
        for n, (r, p) in enumerate(everyone):
            theirs = rows_at(p * 16 + lax.rem(r, 2) * 8, 8, 8)
            copy = remote(
                shared.late_part.at[theirs, :], shared.slabs.at[n],
                shared.slab_send.at[n], shared.slab_recv.at[n], (r, p),
            )
            copy.start()
            copies.append(copy)
        sends.extend(copies)
        yield start + 5
        total = shared.late_part[mine, :]
        for n, copy in enumerate(copies):
            copy.wait_recv()
            total = total + shared.slabs[n]
        shared.slab[...] = total
        copies = []
        for d, device in enumerate(column):
            copy = remote(shared.slab, shared.z_in.at[z], shared.z_send.at[d], shared.z_recv.at[d], device)
            copy.start()
            copies.append(copy)
        sends.extend(copies)
        shared.z_in[z] = total
        yield start + 9
        for copy in copies:
            copy.wait_recv()
        total = shared.z_in[0]
        for d in range(1, 8):
            total = total + shared.z_in[d]
        late_ref[mine, :] = total * (1.0 / ROWS)
        copies = []
        for n, device in enumerate(everyone):
            copy = remote(
                late_ref.at[mine, :], late_ref.at[mine, :], shared.out_send.at[n], shared.out_recv.at[n], device
            )
            copy.start()
            copies.append(copy)
        sends.extend(copies)
        yield start + 14
        for copy in copies:
            copy.wait_recv()

    a, b = halves

    def first():
        yield from gather(a, 0.0, 12.5)
        yield from multiply(a, True, a.gathered, a.part, 16.0, 0.36)
        yield from exchange(a, 23.0, 23.0, 20.0, 12.0)
        yield from multiply(a, False, a.columns, a.part2, 62.0, 0.3)
        yield from reduce(a, 0, 68.0, 16.0)
        yield from early(87.0, 93.0, 98.0, 104.0)

    def second():
        yield 9.0
        yield from gather(b, 13.2, 10.0)
        yield from multiply(b, True, b.gathered, b.part, 27.0, 0.36)
        yield from exchange(b, 34.0, 34.0, 30.0, 11.0)
        yield from multiply(b, False, b.columns, b.part2, 82.0, 0.3)
        yield from reduce(b, H, 88.0, 10.0)
        yield from late(101.5)

    interleave([first(), prepare(), second()])
    for copy in sends:
        copy.wait_send()


def iterate_call(tiles, rows, cols, count, sketch):
    smem = pl.BlockSpec(memory_space=pltpu.SMEM)
    scratch = [make() for _ in range(2) for make in HALF_SCRATCH.values()]
    scratch += [make() for make in SHARED_SCRATCH.values()]
    return pl.pallas_call(
        iterate,
        out_shape=(
            jax.ShapeDtypeStruct((SHARD, K), F32),
            jax.ShapeDtypeStruct((H, K), F32),
            jax.ShapeDtypeStruct((K, H), F32),
        ),
        in_specs=[smem, smem, smem, pl.BlockSpec(memory_space=pl.ANY), whole()],
        out_specs=(whole(), whole(), whole()),
        scratch_shapes=scratch,
        compiler_params=pltpu.CompilerParams(
            collective_id=0, has_side_effects=True, vmem_limit_bytes=VMEM_LIMIT
        ),
        name="iterate",
    )(rows, cols, count, tiles, sketch)


def factor_kernel(early_ref, late_ref, ns_ref, basis_ref, factor_ref, work):
    inverse_t = early_ref[:, H:]
    across = matmul(inverse_t, late_ref[:H, :], ((1,), (0,)))
    i0 = lax.broadcasted_iota(jnp.int32, (H, H), 0)
    i1 = lax.broadcasted_iota(jnp.int32, (H, H), 1)
    work[:, :H] = late_ref[H:, :] - matmul(across, across, ((0,), (0,)))
    work[:, H:] = (i0 == i1).astype(F32)
    factor_ref[:H, :H] = early_ref[:, :H]
    factor_ref[:H, H:] = across
    factor_ref[H:, :H] = jnp.zeros((H, H), F32)
    left = matmul(ns_ref[:, :H], inverse_t, ((1,), (1,)))
    basis_ref[:, :H] = left
    rest = ns_ref[:, H:] - matmul(left, across, ((1,), (0,)))
    for _ in eliminate(work):
        pass
    factor_ref[H:, H:] = jnp.where(i1 >= i0, work[:, :H], 0.0)
    basis_ref[:, H:] = matmul(rest, jnp.where(i0 >= i1, work[:, H:], 0.0), ((1,), (1,)))


def factor_and_basis(early, late, ns):
    return pl.pallas_call(
        factor_kernel,
        out_shape=(
            jax.ShapeDtypeStruct((SHARD, K), F32),
            jax.ShapeDtypeStruct((K, K), F32),
        ),
        in_specs=[whole(), whole(), whole()],
        out_specs=(whole(), whole()),
        scratch_shapes=[vmem((H, 2 * H), F32)],
        compiler_params=pltpu.CompilerParams(vmem_limit_bytes=VMEM_LIMIT),
        name="factor",
    )(early, late, ns)


def body(tiles, tile_rows, tile_cols, tile_counts, sketch):
    ns, early, late = iterate_call(tiles[0, 0], tile_rows[0, 0], tile_cols[0, 0], tile_counts[0], sketch)
    return factor_and_basis(early, late, ns)


def solution(mesh):
    return jax.shard_map(
        body,
        mesh=mesh,
        in_specs=(
            P("row", "col", None, None, None),
            P("row", "col", None),
            P("row", "col", None),
            P("row", "col"),
            P(("row", "col"), None),
        ),
        out_specs=(P(("row", "col"), None), P()),
        check_vma=False,
    )
```

```python
import functools
import heapq

import jax
import jax.numpy as jnp
from jax import lax
from jax.experimental import pallas as pl
from jax.experimental.pallas import tpu as pltpu
from jax.sharding import PartitionSpec as P

TILE = 512
K = 256
H = 128
BR = 12
BC = 12
CAP = 16
SHARD = 384
FULL = 6144
UNIT = 32
TU = TILE // UNIT
PU = 96 // UNIT
ROWS = 98304
STREAMS = 4
Q = SHARD // STREAMS
MESH = pl.DeviceIdType.MESH
HI = lax.Precision.HIGHEST
VMEM_LIMIT = 60 * 1024 * 1024
F32 = jnp.float32
BF16 = jnp.bfloat16
PARTS = 4
PART = SHARD // PARTS
CHAINS = tuple((1 - 2 * (p % 2), p, 4) for p in range(PARTS)) + tuple((2 * (p % 2) - 1, p, 3) for p in range(PARTS))
WIRE = (BF16, BF16, F32, F32)


def vmem(shape, dtype):
    return pltpu.VMEM(shape, dtype)


def dma(n):
    return pltpu.SemaphoreType.DMA((n,))


def whole():
    return pl.BlockSpec(memory_space=pltpu.VMEM)


def flip(i, g):
    x, y = lax.rem(i, 4), lax.div(i, 4)
    if g == 0:
        return i + 1 - 2 * lax.rem(x, 2)
    if g == 1:
        return i + 3 - 2 * x
    if g == 2:
        return i + 4 - 8 * lax.rem(y, 2)
    return i + 12 - 8 * y


def rows_at(start, size, step):
    return pl.ds(pl.multiple_of(start, step), size)


def remote(src, dst, send_sem, recv_sem, device):
    return pltpu.make_async_remote_copy(
        src_ref=src,
        dst_ref=dst,
        send_sem=send_sem,
        recv_sem=recv_sem,
        device_id=device,
        device_id_type=MESH,
    )


def last_step(mask):
    return mask.bit_length() - 1


def first_step(mask):
    return (mask & -mask).bit_length() - 1


def slot_of(n, t):
    return n * 4 + t - 1 if n < PARTS else PARTS * 4 + (n - PARTS) * 3 + t - 1


def interleave(processes):
    queue = []
    for n, process in enumerate(processes):
        heapq.heappush(queue, (next(process), n, process))
    while queue:
        _, n, process = heapq.heappop(queue)
        try:
            heapq.heappush(queue, (next(process), n, process))
        except StopIteration:
            pass


def wide(x):
    return jnp.broadcast_to(x, (8, H))


def matmul(a, b, contract):
    return lax.dot_general(a, b, (contract, ((), ())), precision=HI, preferred_element_type=F32)


def eliminate(work):
    sub = lax.broadcasted_iota(jnp.int32, (8, H), 0)
    panels = H // 8
    below = None
    for p in range(panels):
        j = p * 8
        parts = [work[pl.ds(j, 8), :H], work[pl.ds(j, 8), H:]] if below is None else below
        cols = [wide(parts[0][:, j + k : j + k + 1]) for k in range(8)]
        below = None
        if p + 1 < panels:
            m = j + 8
            rows = work[pl.ds(m, 8), :]
            if p:
                done = work[pl.ds(0, j), :]
                rows = rows - matmul(done[:, m : m + 8], done, ((0,), (0,)))
            below = [rows[:, :H], rows[:, H:]]
            under = [wide(below[0][:, j + k : j + k + 1]) for k in range(8)]
        for i in range(8):
            scale = lax.rsqrt(wide(cols[i][i : i + 1, :]))
            down = jnp.where(sub > i, cols[i] * scale, 0.0)
            if below is not None:
                drop = under[i] * scale
            for k in range(i + 1, 8):
                line = wide(cols[k][i : i + 1, :]) * scale
                cols[k] = cols[k] - down * line
                if below is not None:
                    under[k] = under[k] - drop * line
            for q in range(2):
                line = wide(parts[q][i : i + 1, :]) * scale
                parts[q] = jnp.where(sub == i, line, parts[q] - down * line)
                if below is not None:
                    below[q] = below[q] - drop * line
        for q in range(2):
            work[pl.ds(j, 8), q * H : (q + 1) * H] = parts[q]
        yield


HALF_SCRATCH = dict(
    shard=lambda: vmem((SHARD // UNIT, UNIT, H), BF16),
    gathered=lambda: vmem((FULL // UNIT, UNIT, H), BF16),
    ag_send=lambda: dma(1),
    ag_recv=lambda: dma(STREAMS * 15),
    acc=lambda: vmem((CAP + 1, TILE, H), F32),
    part=lambda: vmem((FULL, H), F32),
    pair_buf=lambda: vmem((8 * PARTS, PART, H), F32),
    sums=lambda: vmem((7 * PARTS, PART, H), F32),
    landed=lambda: vmem((7 * PARTS, PART, H), F32),
    pair_send=lambda: dma(1),
    pair_recv=lambda: dma(8 * PARTS),
    chain_send=lambda: dma(1),
    chain_recv=lambda: dma(7 * PARTS),
    own=lambda: vmem((SHARD // UNIT, UNIT, H), BF16),
    columns=lambda: vmem((FULL // UNIT, UNIT, H), BF16),
    gather_send=lambda: dma(1),
    gather_recv=lambda: dma(7 * PARTS),
    twin_send=lambda: dma(1),
    twin_recv=lambda: dma(1),
    part2=lambda: vmem((FULL, H), BF16),
    land0=lambda: vmem((STREAMS * 8, Q, H), BF16),
    land1=lambda: vmem((STREAMS * 4, Q, H), WIRE[1]),
    land2=lambda: vmem((STREAMS * 3, Q, H), F32),
    acc2=lambda: vmem((STREAMS * 8, Q, H), F32),
    wire1=lambda: vmem((STREAMS * 4, Q, H), BF16),
    rs_send=lambda: dma(2),
    rs_recv=lambda: dma(STREAMS * 15),
)

SHARED_SCRATCH = dict(
    tiles=lambda: vmem((CAP, TILE, TILE), BF16),
    tile_sem=lambda: dma(CAP),
    work=lambda: vmem((H, 2 * H), F32),
    early_part=lambda: vmem((H, H), F32),
    early_in=lambda: vmem((16, 8, H), F32),
    early_row=lambda: vmem((16, 8, H), F32),
    early_slab=lambda: vmem((8, H), F32),
    early_sum=lambda: vmem((8, H), F32),
    early_gram=lambda: vmem((H, H), F32),
    early_send=lambda: dma(3),
    early_recv=lambda: dma(3),
    late_part=lambda: vmem((K, H), F32),
    slabs=lambda: vmem((31, 8, H), F32),
    slab=lambda: vmem((8, H), F32),
    slab_send=lambda: dma(1),
    slab_recv=lambda: dma(1),
    z_in=lambda: vmem((8, 8, H), F32),
    z_send=lambda: dma(1),
    z_recv=lambda: dma(1),
    out_send=lambda: dma(1),
    out_recv=lambda: dma(1),
)


class Refs:
    pass


def named(names, refs):
    out = Refs()
    for name, ref in zip(names, refs):
        setattr(out, name, ref)
    return out


def iterate(rows_ref, cols_ref, count_ref, tiles_ref, sketch_ref, ns_ref, early_ref, late_ref, *scratch):
    nh = len(HALF_SCRATCH)
    halves = [named(HALF_SCRATCH, scratch[i * nh : (i + 1) * nh]) for i in (0, 1)]
    shared = named(SHARED_SCRATCH, scratch[2 * nh :])

    row, me = lax.axis_index("row"), lax.axis_index("col")
    z, core = lax.div(row, 2), lax.rem(row, 2)
    other = row + 1 - 2 * core
    twin = (other, me)
    near = [(row, flip(me, g)) for g in range(4)]
    plane = [lax.rem(me + d, 16) for d in range(1, 16)]

    def ring(d):
        return lax.rem(z + d + 8, 8)

    side = {1: (2 * ring(1) + core, me), -1: (2 * ring(-1) + core, me)}
    column = [(2 * ring(d) + core, me) for d in range(1, 8)]
    everyone = [twin] + [(r, p) for p in plane for r in (row, other)]
    line = [(lax.rem(row + d, 16), me) for d in range(1, 16)]

    loads = []
    for s in range(CAP):
        load = pltpu.make_async_copy(tiles_ref.at[s], shared.tiles.at[s], shared.tile_sem.at[s])
        load.start()
        loads.append(load)
    for i, half in enumerate(halves):
        half.shard[...] = sketch_ref[:, i * H : (i + 1) * H].reshape(SHARD // UNIT, UNIT, H)

    barrier = pltpu.get_barrier_semaphore()
    greeted = everyone[1:] + line
    for device in greeted:
        pl.semaphore_signal(barrier, inc=1, device_id=device, device_id_type=MESH)
    pl.semaphore_wait(barrier, len(greeted))

    plan = {}

    def landed_all(view, sem):
        remote(view, view, sem, sem, twin).wait_recv()

    def left_all(view, sem):
        remote(view, view, sem, sem, twin).wait_send()

    def places(targets):
        to = [targets[t] for t in range(CAP)]
        count = count_ref[0]
        before, ends = [], []
        for s in range(CAP):
            at = jnp.int32(0)
            for t in range(s):
                at = jnp.where(to[t] == to[s], t + 1, at)
            before.append(at)
        for b in range(BR):
            at = jnp.int32(0)
            for t in range(CAP):
                at = jnp.where((to[t] == b) & (t < count), t + 1, at)
            ends.append(at)
        return before, ends

    def gather(half, start, flow):
        copies = {}
        half.gathered[pl.ds(me * (SHARD // UNIT), SHARD // UNIT)] = half.shard[...]

        def block_at(k, mask):
            block = me
            for s in range(4):
                if mask >> s & 1:
                    block = flip(block, (k + s) % 4)
            return pl.ds(block * (SHARD // UNIT) + k * (Q // UNIT), Q // UNIT)

        def forward(k, mask, s):
            at = block_at(k, mask)
            src = half.shard.at[pl.ds(k * (Q // UNIT), Q // UNIT)] if mask == 0 else half.gathered.at[at]
            slot = k * 15 + (mask | 1 << s) - 1
            copy = remote(
                src, half.gathered.at[at], half.ag_send.at[0], half.ag_recv.at[slot], near[(k + s) % 4]
            )
            copy.start()
            copies[k, mask | 1 << s] = copy

        for s in range(4):
            for k in range(STREAMS):
                forward(k, 0, s)
        masks = sorted(range(1, 16), key=lambda m: (m.bit_count(), last_step(m), m))
        n = 0
        for mask in masks:
            for k in range(STREAMS):
                yield start + 3 + flow * n / 60
                n += 1
                copies[k, mask].wait_recv()
                for s in range(last_step(mask) + 1, 4):
                    forward(k, mask, s)

    def multiply(half, transposed, source, result, start, per_tile):
        src = rows_ref if transposed else cols_ref
        before, ends = plan[transposed]
        dims = (((0,), (0,)), ((), ())) if transposed else (((1,), (0,)), ((), ()))
        for s in range(CAP):
            yield start + per_tile * s
            if loads[s] is not None:
                loads[s].wait()
                loads[s] = None
            block = source[pl.ds(src[s] * TU, TU)].reshape(TILE, H)
            for u in range(2):
                part = pl.ds(u * 256, 256)
                tile = shared.tiles[s, :, part] if transposed else shared.tiles[s, part, :]
                half.acc[s + 1, part, :] = half.acc[before[s], part, :] + lax.dot_general(
                    tile, block, dims, preferred_element_type=F32
                )
        for b in range(BR):
            yield start + per_tile * CAP + 0.08 * b
            result[pl.ds(b * TILE, TILE), :] = half.acc[ends[b]].astype(result.dtype)

    def exchange(half, start, ring_start, reduce_flow, gather_flow):
        yield start
        order = []
        for t in range(1, 5):
            for direction, part, hops in CHAINS:
                if t <= hops:
                    item = (direction * (hops + 1 - t) % 8, part)
                    if item not in order:
                        order.append(item)
        order += [(0, part) for part in range(PARTS)]
        pair = {}
        for d, part in order:
            slot = d * PARTS + part
            theirs = rows_at((2 * ring(d) + 1 - core) * SHARD + part * PART, PART, PART)
            pair[d, part] = remote(
                half.part.at[theirs, :], half.pair_buf.at[slot],
                half.pair_send.at[0], half.pair_recv.at[slot], twin,
            )
            pair[d, part].start()
        arrived = set()

        def chip_sum(d, part):
            d = d % 8
            slot = d * PARTS + part
            if (d, part) not in arrived:
                pair[d, part].wait_recv()
                arrived.add((d, part))
            mine = rows_at((2 * ring(d) + core) * SHARD + part * PART, PART, PART)
            return half.part[mine, :] + half.pair_buf[slot]

        last = {}
        n_sent = 0
        for t in range(1, 5):
            for n, (direction, part, hops) in enumerate(CHAINS):
                if t > hops:
                    continue
                yield ring_start + 2 + reduce_flow * n_sent / (7 * PARTS)
                n_sent += 1
                slot = slot_of(n, t)
                value = chip_sum(direction * (hops + 1 - t), part)
                if t > 1:
                    last[n].wait_recv()
                    value = value + half.landed[slot - 1]
                half.sums[slot] = value
                copy = remote(
                    half.sums.at[slot], half.landed.at[slot],
                    half.chain_send.at[0], half.chain_recv.at[slot], side[direction],
                )
                copy.start()
                last[n] = copy
        begin = ring_start + 3 + reduce_flow
        moving = {}

        def spread(src, at):
            copy = remote(src, half.columns.at[at], half.twin_send.at[0], half.twin_recv.at[0], twin)
            copy.start()

        def pass_on(src, at, n, t):
            slot = slot_of(n, t + 1)
            copy = remote(
                src, half.columns.at[at],
                half.gather_send.at[0], half.gather_recv.at[slot], side[CHAINS[n][0]],
            )
            copy.start()
            moving[n] = copy

        for part in range(PARTS):
            yield begin + 0.1 * part
            value = chip_sum(0, part)
            for n in (part + PARTS, part):
                last[n].wait_recv()
                value = value + half.landed[slot_of(n, CHAINS[n][2])]
            local = pl.ds(part * PU, PU)
            rounded = value.astype(BF16).reshape(PU, UNIT, H)
            half.own[local] = rounded
            at = pl.ds((row * PARTS + part) * PU, PU)
            half.columns[at] = rounded
            for n in range(2 * PARTS):
                if CHAINS[n][1] == part:
                    pass_on(half.own.at[local], at, n, 0)
            spread(half.own.at[local], at)
        n_got = 0
        for t in range(1, 5):
            for n, (direction, part, hops) in enumerate(CHAINS):
                if t > hops:
                    continue
                yield begin + 2 + gather_flow * n_got / (7 * PARTS)
                n_got += 1
                moving[n].wait_recv()
                at = pl.ds(((2 * ring(-direction * t) + core) * PARTS + part) * PU, PU)
                if t < hops:
                    pass_on(half.columns.at[at], at, n, t)
                spread(half.columns.at[at], at)
        yield begin + 3 + gather_flow
        landed_all(half.columns.at[pl.ds(0, 8 * PARTS * PU)], half.twin_recv.at[0])

    def reduce(half, lane, start, flow):
        yield start
        copies = {}

        def block_at(k, mask):
            block = me
            for s in range(4):
                if mask >> s & 1:
                    block = flip(block, (k + s) % 4)
            return rows_at(block * SHARD + k * Q, Q, 16)

        def landing(k, s, mask):
            if s == 0:
                return half.land0.at[k * 8 + mask // 2]
            if s == 1:
                return half.land1.at[k * 4 + mask // 4]
            return half.land2.at[k * 3 + (mask // 8 if s == 2 else 2)]

        def send(k, mask):
            s = first_step(mask)
            if s == 0:
                src = half.part2.at[block_at(k, mask), :]
            elif WIRE[s] == BF16:
                half.wire1[k * 4 + mask // 4] = half.acc2[k * 8 + mask // 2].astype(BF16)
                src = half.wire1.at[k * 4 + mask // 4]
            else:
                src = half.acc2.at[k * 8 + mask // 2]
            slot = k * 15 + mask - 1
            copy = remote(
                src, landing(k, s, mask ^ (1 << s)), half.rs_send.at[s // 2], half.rs_recv.at[slot],
                near[(k + s) % 4],
            )
            copy.start()
            copies[k, mask] = copy

        def urgency(mask):
            rest = mask & ~1
            return (first_step(rest) if rest else 4, -mask)

        for mask in sorted((m for m in range(16) if m & 1), key=urgency):
            for k in range(STREAMS):
                send(k, mask)
        n = 0
        entries = sorted((m for m in range(16) if not m & 1), key=lambda m: (first_step(m) if m else 4, -m))
        for mask in entries:
            steps = first_step(mask) if mask else 4
            for k in range(STREAMS):
                yield start + 2.5 + flow * n / 32
                n += 1
                value = half.part2[block_at(k, mask), :].astype(F32)
                for s in range(steps):
                    copies[k, mask | 1 << s].wait_recv()
                    value = value + landing(k, s, mask)[...].astype(F32)
                if mask:
                    half.acc2[k * 8 + mask // 2] = value
                    send(k, mask)
                else:
                    ns_ref[pl.ds(k * Q, Q), pl.ds(lane, H)] = value

    def prepare():
        yield 0.5
        for half in halves:
            half.acc[0] = jnp.zeros((TILE, H), F32)
        plan[True] = places(cols_ref)
        plan[False] = places(rows_ref)

    def early(start, plane_at, line_at, eliminate_at):
        yield start
        rows = ns_ref[:, :H]
        shared.early_part[...] = lax.dot_general(
            rows, rows, (((0,), (0,)), ((), ())), precision=HI, preferred_element_type=F32
        )
        mine = rows_at(me * 8, 8, 8)
        for d, p in enumerate(plane):
            copy = remote(
                shared.early_part.at[rows_at(p * 8, 8, 8), :], shared.early_in.at[d],
                shared.early_send.at[0], shared.early_recv.at[0], (row, p),
            )
            copy.start()
        yield plane_at
        total = shared.early_part[mine, :]
        landed_all(shared.early_in.at[pl.ds(0, 15)], shared.early_recv.at[0])
        for d in range(15):
            total = total + shared.early_in[d]
        shared.early_slab[...] = total
        shared.early_row[row] = total
        for d, device in enumerate(line):
            copy = remote(
                shared.early_slab, shared.early_row.at[row],
                shared.early_send.at[1], shared.early_recv.at[1], device,
            )
            copy.start()
        yield line_at
        landed_all(shared.early_in.at[pl.ds(0, 15)], shared.early_recv.at[1])
        total = shared.early_row[0]
        for d in range(1, 16):
            total = total + shared.early_row[d]
        total = total * (1.0 / ROWS)
        shared.early_sum[...] = total
        shared.early_gram[mine, :] = total
        for d, p in enumerate(plane):
            copy = remote(
                shared.early_sum, shared.early_gram.at[mine, :],
                shared.early_send.at[2], shared.early_recv.at[2], (row, p),
            )
            copy.start()
        yield eliminate_at
        landed_all(shared.early_in.at[pl.ds(0, 15)], shared.early_recv.at[2])
        i0 = lax.broadcasted_iota(jnp.int32, (H, H), 0)
        i1 = lax.broadcasted_iota(jnp.int32, (H, H), 1)
        shared.work[:, :H] = shared.early_gram[...]
        shared.work[:, H:] = (i0 == i1).astype(F32)
        for n, _ in enumerate(eliminate(shared.work)):
            yield eliminate_at + 0.4 * n
        early_ref[:, :H] = jnp.where(i1 >= i0, shared.work[:, :H], 0.0)
        early_ref[:, H:] = jnp.where(i0 >= i1, shared.work[:, H:], 0.0)

    def late(start):
        yield start
        shared.late_part[...] = lax.dot_general(
            ns_ref[...], ns_ref[:, H:], (((0,), (0,)), ((), ())), precision=HI, preferred_element_type=F32
        )
        mine = rows_at(me * 16 + core * 8, 8, 8)
        for n, (r, p) in enumerate(everyone):
            theirs = rows_at(p * 16 + lax.rem(r, 2) * 8, 8, 8)
            copy = remote(
                shared.late_part.at[theirs, :], shared.slabs.at[n],
                shared.slab_send.at[0], shared.slab_recv.at[0], (r, p),
            )
            copy.start()
        yield start + 5
        total = shared.late_part[mine, :]
        landed_all(shared.slabs, shared.slab_recv.at[0])
        for n in range(31):
            total = total + shared.slabs[n]
        shared.slab[...] = total
        for d, device in enumerate(column):
            copy = remote(shared.slab, shared.z_in.at[z], shared.z_send.at[0], shared.z_recv.at[0], device)
            copy.start()
        shared.z_in[z] = total
        yield start + 9
        landed_all(shared.z_in.at[pl.ds(0, 7)], shared.z_recv.at[0])
        total = shared.z_in[0]
        for d in range(1, 8):
            total = total + shared.z_in[d]
        late_ref[mine, :] = total * (1.0 / ROWS)
        for n, device in enumerate(everyone):
            copy = remote(
                late_ref.at[mine, :], late_ref.at[mine, :], shared.out_send.at[0], shared.out_recv.at[0], device
            )
            copy.start()
        yield start + 14
        landed_all(shared.slabs, shared.out_recv.at[0])

    a, b = halves

    def first():
        yield from gather(a, 0.0, 12.5)
        yield from multiply(a, True, a.gathered, a.part, 16.0, 0.36)
        yield from exchange(a, 23.0, 23.0, 20.0, 12.0)
        yield from multiply(a, False, a.columns, a.part2, 62.0, 0.3)
        yield from reduce(a, 0, 68.0, 16.0)
        yield from early(87.0, 93.0, 98.0, 104.0)

    def second():
        yield 9.0
        yield from gather(b, 13.2, 10.0)
        yield from multiply(b, True, b.gathered, b.part, 27.0, 0.36)
        yield from exchange(b, 34.0, 34.0, 30.0, 11.0)
        yield from multiply(b, False, b.columns, b.part2, 82.0, 0.3)
        yield from reduce(b, H, 88.0, 10.0)
        yield from late(101.5)

    interleave([first(), prepare(), second()])
    for half in halves:
        left_all(half.gathered.at[pl.ds(0, 15 * SHARD // UNIT)], half.ag_send.at[0])
        left_all(half.pair_buf, half.pair_send.at[0])
        left_all(half.sums, half.chain_send.at[0])
        left_all(half.columns.at[pl.ds(0, 7 * PARTS * PU)], half.gather_send.at[0])
        left_all(half.columns.at[pl.ds(0, 8 * PARTS * PU)], half.twin_send.at[0])
        left_all(half.columns.at[pl.ds(0, 12 * STREAMS * PU)], half.rs_send.at[0])
        left_all(half.acc2.at[pl.ds(0, 3 * STREAMS)], half.rs_send.at[1])
    for n in range(3):
        left_all(shared.early_in.at[pl.ds(0, 15)], shared.early_send.at[n])
    left_all(shared.slabs, shared.slab_send.at[0])
    left_all(shared.z_in.at[pl.ds(0, 7)], shared.z_send.at[0])
    left_all(shared.slabs, shared.out_send.at[0])


def iterate_call(tiles, rows, cols, count, sketch):
    smem = pl.BlockSpec(memory_space=pltpu.SMEM)
    scratch = [make() for _ in range(2) for make in HALF_SCRATCH.values()]
    scratch += [make() for make in SHARED_SCRATCH.values()]
    return pl.pallas_call(
        iterate,
        out_shape=(
            jax.ShapeDtypeStruct((SHARD, K), F32),
            jax.ShapeDtypeStruct((H, K), F32),
            jax.ShapeDtypeStruct((K, H), F32),
        ),
        in_specs=[smem, smem, smem, pl.BlockSpec(memory_space=pl.ANY), whole()],
        out_specs=(whole(), whole(), whole()),
        scratch_shapes=scratch,
        compiler_params=pltpu.CompilerParams(
            collective_id=0, has_side_effects=True, vmem_limit_bytes=VMEM_LIMIT
        ),
        name="iterate",
    )(rows, cols, count, tiles, sketch)


def factor_kernel(early_ref, late_ref, ns_ref, basis_ref, factor_ref, work):
    inverse_t = early_ref[:, H:]
    across = matmul(inverse_t, late_ref[:H, :], ((1,), (0,)))
    i0 = lax.broadcasted_iota(jnp.int32, (H, H), 0)
    i1 = lax.broadcasted_iota(jnp.int32, (H, H), 1)
    work[:, :H] = late_ref[H:, :] - matmul(across, across, ((0,), (0,)))
    work[:, H:] = (i0 == i1).astype(F32)
    factor_ref[:H, :H] = early_ref[:, :H]
    factor_ref[:H, H:] = across
    factor_ref[H:, :H] = jnp.zeros((H, H), F32)
    left = matmul(ns_ref[:, :H], inverse_t, ((1,), (1,)))
    basis_ref[:, :H] = left
    rest = ns_ref[:, H:] - matmul(left, across, ((1,), (0,)))
    for _ in eliminate(work):
        pass
    factor_ref[H:, H:] = jnp.where(i1 >= i0, work[:, :H], 0.0)
    basis_ref[:, H:] = matmul(rest, jnp.where(i0 >= i1, work[:, H:], 0.0), ((1,), (1,)))


def factor_and_basis(early, late, ns):
    return pl.pallas_call(
        factor_kernel,
        out_shape=(
            jax.ShapeDtypeStruct((SHARD, K), F32),
            jax.ShapeDtypeStruct((K, K), F32),
        ),
        in_specs=[whole(), whole(), whole()],
        out_specs=(whole(), whole()),
        scratch_shapes=[vmem((H, 2 * H), F32)],
        compiler_params=pltpu.CompilerParams(vmem_limit_bytes=VMEM_LIMIT),
        name="factor",
    )(early, late, ns)


def body(tiles, tile_rows, tile_cols, tile_counts, sketch):
    ns, early, late = iterate_call(tiles[0, 0], tile_rows[0, 0], tile_cols[0, 0], tile_counts[0], sketch)
    return factor_and_basis(early, late, ns)


def solution(mesh):
    return jax.shard_map(
        body,
        mesh=mesh,
        in_specs=(
            P("row", "col", None, None, None),
            P("row", "col", None),
            P("row", "col", None),
            P("row", "col"),
            P(("row", "col"), None),
        ),
        out_specs=(P(("row", "col"), None), P()),
        check_vma=False,
    )
```

```python
import functools
import heapq

import jax
import jax.numpy as jnp
from jax import lax
from jax.experimental import pallas as pl
from jax.experimental.pallas import tpu as pltpu
from jax.sharding import PartitionSpec as P

TILE = 512
K = 256
H = 128
BR = 12
BC = 12
CAP = 16
SHARD = 384
FULL = 6144
UNIT = 32
TU = TILE // UNIT
PU = 96 // UNIT
ROWS = 98304
STREAMS = 4
Q = SHARD // STREAMS
MESH = pl.DeviceIdType.MESH
HI = lax.Precision.HIGHEST
VMEM_LIMIT = 60 * 1024 * 1024
F32 = jnp.float32
BF16 = jnp.bfloat16
PARTS = 4
PART = SHARD // PARTS
CHAINS = tuple((1 - 2 * (p % 2), p, 4) for p in range(PARTS)) + tuple((2 * (p % 2) - 1, p, 3) for p in range(PARTS))
WIRE = (BF16, BF16, F32, F32)


def vmem(shape, dtype):
    return pltpu.VMEM(shape, dtype)


def dma(n):
    return pltpu.SemaphoreType.DMA((n,))


def whole():
    return pl.BlockSpec(memory_space=pltpu.VMEM)


def flip(i, g):
    x, y = lax.rem(i, 4), lax.div(i, 4)
    if g == 0:
        return i + 1 - 2 * lax.rem(x, 2)
    if g == 1:
        return i + 3 - 2 * x
    if g == 2:
        return i + 4 - 8 * lax.rem(y, 2)
    return i + 12 - 8 * y


def rows_at(start, size, step):
    return pl.ds(pl.multiple_of(start, step), size)


def remote(src, dst, send_sem, recv_sem, device):
    return pltpu.make_async_remote_copy(
        src_ref=src,
        dst_ref=dst,
        send_sem=send_sem,
        recv_sem=recv_sem,
        device_id=device,
        device_id_type=MESH,
    )


def last_step(mask):
    return mask.bit_length() - 1


def first_step(mask):
    return (mask & -mask).bit_length() - 1


def slot_of(n, t):
    return n * 4 + t - 1 if n < PARTS else PARTS * 4 + (n - PARTS) * 3 + t - 1


def interleave(processes):
    queue = []
    for n, process in enumerate(processes):
        heapq.heappush(queue, (next(process), n, process))
    while queue:
        _, n, process = heapq.heappop(queue)
        try:
            heapq.heappush(queue, (next(process), n, process))
        except StopIteration:
            pass


def wide(x):
    return jnp.broadcast_to(x, (8, H))


def matmul(a, b, contract):
    return lax.dot_general(a, b, (contract, ((), ())), precision=HI, preferred_element_type=F32)


def eliminate(work):
    sub = lax.broadcasted_iota(jnp.int32, (8, H), 0)
    panels = H // 8
    below = None
    for p in range(panels):
        j = p * 8
        parts = [work[pl.ds(j, 8), :H], work[pl.ds(j, 8), H:]] if below is None else below
        cols = [wide(parts[0][:, j + k : j + k + 1]) for k in range(8)]
        below = None
        if p + 1 < panels:
            m = j + 8
            rows = work[pl.ds(m, 8), :]
            if p:
                done = work[pl.ds(0, j), :]
                rows = rows - matmul(done[:, m : m + 8], done, ((0,), (0,)))
            below = [rows[:, :H], rows[:, H:]]
            under = [wide(below[0][:, j + k : j + k + 1]) for k in range(8)]
        for i in range(8):
            scale = lax.rsqrt(wide(cols[i][i : i + 1, :]))
            down = jnp.where(sub > i, cols[i] * scale, 0.0)
            if below is not None:
                drop = under[i] * scale
            for k in range(i + 1, 8):
                line = wide(cols[k][i : i + 1, :]) * scale
                cols[k] = cols[k] - down * line
                if below is not None:
                    under[k] = under[k] - drop * line
            for q in range(2):
                line = wide(parts[q][i : i + 1, :]) * scale
                parts[q] = jnp.where(sub == i, line, parts[q] - down * line)
                if below is not None:
                    below[q] = below[q] - drop * line
        for q in range(2):
            work[pl.ds(j, 8), q * H : (q + 1) * H] = parts[q]
        yield


HALF_SCRATCH = dict(
    shard=lambda: vmem((SHARD // UNIT, UNIT, H), BF16),
    gathered=lambda: vmem((FULL // UNIT, UNIT, H), BF16),
    ag_send=lambda: dma(1),
    ag_recv=lambda: dma(STREAMS * 15),
    acc=lambda: vmem((CAP + 1, TILE, H), F32),
    part=lambda: vmem((FULL, H), F32),
    pair_buf=lambda: vmem((8 * PARTS, PART, H), F32),
    sums=lambda: vmem((7 * PARTS, PART, H), F32),
    landed=lambda: vmem((7 * PARTS, PART, H), F32),
    pair_send=lambda: dma(1),
    pair_recv=lambda: dma(8 * PARTS),
    chain_send=lambda: dma(1),
    chain_recv=lambda: dma(7 * PARTS),
    own=lambda: vmem((SHARD // UNIT, UNIT, H), BF16),
    columns=lambda: vmem((FULL // UNIT, UNIT, H), BF16),
    gather_send=lambda: dma(1),
    gather_recv=lambda: dma(7 * PARTS),
    twin_send=lambda: dma(1),
    twin_recv=lambda: dma(1),
    part2=lambda: vmem((FULL, H), BF16),
    land0=lambda: vmem((STREAMS * 8, Q, H), BF16),
    land1=lambda: vmem((STREAMS * 4, Q, H), WIRE[1]),
    land2=lambda: vmem((STREAMS * 3, Q, H), F32),
    acc2=lambda: vmem((STREAMS * 8, Q, H), F32),
    wire1=lambda: vmem((STREAMS * 4, Q, H), BF16),
    rs_send=lambda: dma(2),
    rs_recv=lambda: dma(STREAMS * 15),
)

SHARED_SCRATCH = dict(
    tiles=lambda: vmem((CAP, TILE, TILE), BF16),
    tile_sem=lambda: dma(CAP),
    work=lambda: vmem((H, 2 * H), F32),
    early_part=lambda: vmem((H, H), F32),
    early_in=lambda: vmem((16, 8, H), F32),
    early_row=lambda: vmem((16, 8, H), F32),
    early_slab=lambda: vmem((8, H), F32),
    early_sum=lambda: vmem((8, H), F32),
    early_gram=lambda: vmem((H, H), F32),
    early_send=lambda: dma(3),
    early_recv=lambda: dma(3),
    late_part=lambda: vmem((K, H), F32),
    slabs=lambda: vmem((31, 8, H), F32),
    slab=lambda: vmem((8, H), F32),
    slab_send=lambda: dma(1),
    slab_recv=lambda: dma(1),
    z_in=lambda: vmem((8, 8, H), F32),
    z_send=lambda: dma(1),
    z_recv=lambda: dma(1),
    out_send=lambda: dma(1),
    out_recv=lambda: dma(1),
)


class Refs:
    pass


def named(names, refs):
    out = Refs()
    for name, ref in zip(names, refs):
        setattr(out, name, ref)
    return out


def iterate(rows_ref, cols_ref, count_ref, tiles_ref, sketch_ref, ns_ref, early_ref, late_ref, *scratch):
    nh = len(HALF_SCRATCH)
    halves = [named(HALF_SCRATCH, scratch[i * nh : (i + 1) * nh]) for i in (0, 1)]
    shared = named(SHARED_SCRATCH, scratch[2 * nh :])

    row, me = lax.axis_index("row"), lax.axis_index("col")
    z, core = lax.div(row, 2), lax.rem(row, 2)
    other = row + 1 - 2 * core
    twin = (other, me)
    near = [(row, flip(me, g)) for g in range(4)]
    plane = [lax.rem(me + d, 16) for d in range(1, 16)]

    def ring(d):
        return lax.rem(z + d + 8, 8)

    side = {1: (2 * ring(1) + core, me), -1: (2 * ring(-1) + core, me)}
    column = [(2 * ring(d) + core, me) for d in range(1, 8)]
    everyone = [twin] + [(r, p) for p in plane for r in (row, other)]
    line = [(lax.rem(row + d, 16), me) for d in range(1, 16)]

    loads = []
    for s in range(CAP):
        load = pltpu.make_async_copy(tiles_ref.at[s], shared.tiles.at[s], shared.tile_sem.at[s])
        load.start()
        loads.append(load)
    for i, half in enumerate(halves):
        half.shard[...] = sketch_ref[:, i * H : (i + 1) * H].reshape(SHARD // UNIT, UNIT, H)

    barrier = pltpu.get_barrier_semaphore()
    greeted = everyone[1:] + line
    for device in greeted:
        pl.semaphore_signal(barrier, inc=1, device_id=device, device_id_type=MESH)
    pl.semaphore_wait(barrier, len(greeted))

    plan = {}

    def landed_all(view, sem):
        remote(view, view, sem, sem, twin).wait_recv()

    def left_all(view, sem):
        remote(view, view, sem, sem, twin).wait_send()

    def places(targets):
        to = [targets[t] for t in range(CAP)]
        count = count_ref[0]
        before, ends = [], []
        for s in range(CAP):
            at = jnp.int32(0)
            for t in range(s):
                at = jnp.where(to[t] == to[s], t + 1, at)
            before.append(at)
        for b in range(BR):
            at = jnp.int32(0)
            for t in range(CAP):
                at = jnp.where((to[t] == b) & (t < count), t + 1, at)
            ends.append(at)
        return before, ends

    def gather(half, start, flow):
        copies = {}
        half.gathered[pl.ds(me * (SHARD // UNIT), SHARD // UNIT)] = half.shard[...]

        def block_at(k, mask):
            block = me
            for s in range(4):
                if mask >> s & 1:
                    block = flip(block, (k + s) % 4)
            return pl.ds(block * (SHARD // UNIT) + k * (Q // UNIT), Q // UNIT)

        def forward(k, mask, s):
            at = block_at(k, mask)
            src = half.shard.at[pl.ds(k * (Q // UNIT), Q // UNIT)] if mask == 0 else half.gathered.at[at]
            slot = k * 15 + (mask | 1 << s) - 1
            copy = remote(
                src, half.gathered.at[at], half.ag_send.at[0], half.ag_recv.at[slot], near[(k + s) % 4]
            )
            copy.start()
            copies[k, mask | 1 << s] = copy

        for s in range(4):
            for k in range(STREAMS):
                forward(k, 0, s)
        masks = sorted(range(1, 16), key=lambda m: (m.bit_count(), last_step(m), m))
        n = 0
        for mask in masks:
            for k in range(STREAMS):
                yield start + 3 + flow * n / 60
                n += 1
                copies[k, mask].wait_recv()
                for s in range(last_step(mask) + 1, 4):
                    forward(k, mask, s)

    def multiply(half, transposed, source, result, start, per_tile):
        src = rows_ref if transposed else cols_ref
        before, ends = plan[transposed]
        dims = (((0,), (0,)), ((), ())) if transposed else (((1,), (0,)), ((), ()))
        for s in range(CAP):
            yield start + per_tile * s
            if loads[s] is not None:
                loads[s].wait()
                loads[s] = None
            block = source[pl.ds(src[s] * TU, TU)].reshape(TILE, H)
            for u in range(2):
                part = pl.ds(u * 256, 256)
                tile = shared.tiles[s, :, part] if transposed else shared.tiles[s, part, :]
                half.acc[s + 1, part, :] = half.acc[before[s], part, :] + lax.dot_general(
                    tile, block, dims, preferred_element_type=F32
                )
        for b in range(BR):
            yield start + per_tile * CAP + 0.08 * b
            result[pl.ds(b * TILE, TILE), :] = half.acc[ends[b]].astype(result.dtype)

    def exchange(half, start, reduce_at, own_at, gather_at, twins_at):
        yield start
        order = []
        for t in range(1, 5):
            for direction, part, hops in CHAINS:
                if t <= hops:
                    item = (direction * (hops + 1 - t) % 8, part)
                    if item not in order:
                        order.append(item)
        order += [(0, part) for part in range(PARTS)]
        pair = {}
        for d, part in order:
            slot = d * PARTS + part
            theirs = rows_at((2 * ring(d) + 1 - core) * SHARD + part * PART, PART, PART)
            pair[d, part] = remote(
                half.part.at[theirs, :], half.pair_buf.at[slot],
                half.pair_send.at[0], half.pair_recv.at[slot], twin,
            )
            pair[d, part].start()
        arrived = set()

        def chip_sum(d, part):
            d = d % 8
            slot = d * PARTS + part
            if (d, part) not in arrived:
                pair[d, part].wait_recv()
                arrived.add((d, part))
            mine = rows_at((2 * ring(d) + core) * SHARD + part * PART, PART, PART)
            return half.part[mine, :] + half.pair_buf[slot]

        last = {}
        for t in range(1, 5):
            for n, (direction, part, hops) in enumerate(CHAINS):
                if t > hops:
                    continue
                yield reduce_at[t - 1] + 0.3 * n
                slot = slot_of(n, t)
                value = chip_sum(direction * (hops + 1 - t), part)
                if t > 1:
                    last[n].wait_recv()
                    value = value + half.landed[slot - 1]
                half.sums[slot] = value
                copy = remote(
                    half.sums.at[slot], half.landed.at[slot],
                    half.chain_send.at[0], half.chain_recv.at[slot], side[direction],
                )
                copy.start()
                last[n] = copy
        moving = {}

        def spread(src, at):
            copy = remote(src, half.columns.at[at], half.twin_send.at[0], half.twin_recv.at[0], twin)
            copy.start()

        def pass_on(src, at, n, t):
            slot = slot_of(n, t + 1)
            copy = remote(
                src, half.columns.at[at],
                half.gather_send.at[0], half.gather_recv.at[slot], side[CHAINS[n][0]],
            )
            copy.start()
            moving[n] = copy

        for part in range(PARTS):
            yield own_at + 0.02 * part
            value = chip_sum(0, part)
            for n in (part + PARTS, part):
                last[n].wait_recv()
                value = value + half.landed[slot_of(n, CHAINS[n][2])]
            local = pl.ds(part * PU, PU)
            rounded = value.astype(BF16).reshape(PU, UNIT, H)
            half.own[local] = rounded
            at = pl.ds((row * PARTS + part) * PU, PU)
            half.columns[at] = rounded
            for n in range(2 * PARTS):
                if CHAINS[n][1] == part:
                    pass_on(half.own.at[local], at, n, 0)
            spread(half.own.at[local], at)
        for t in range(1, 5):
            for n, (direction, part, hops) in enumerate(CHAINS):
                if t > hops:
                    continue
                yield gather_at[t - 1] + 0.3 * n
                moving[n].wait_recv()
                at = pl.ds(((2 * ring(-direction * t) + core) * PARTS + part) * PU, PU)
                if t < hops:
                    pass_on(half.columns.at[at], at, n, t)
                spread(half.columns.at[at], at)
        yield twins_at
        landed_all(half.columns.at[pl.ds(0, 8 * PARTS * PU)], half.twin_recv.at[0])

    def reduce(half, lane, start, at, flow):
        yield start
        copies = {}

        def block_at(k, mask):
            block = me
            for s in range(4):
                if mask >> s & 1:
                    block = flip(block, (k + s) % 4)
            return rows_at(block * SHARD + k * Q, Q, 16)

        def landing(k, s, mask):
            if s == 0:
                return half.land0.at[k * 8 + mask // 2]
            if s == 1:
                return half.land1.at[k * 4 + mask // 4]
            return half.land2.at[k * 3 + (mask // 8 if s == 2 else 2)]

        def send(k, mask):
            s = first_step(mask)
            if s == 0:
                src = half.part2.at[block_at(k, mask), :]
            elif WIRE[s] == BF16:
                half.wire1[k * 4 + mask // 4] = half.acc2[k * 8 + mask // 2].astype(BF16)
                src = half.wire1.at[k * 4 + mask // 4]
            else:
                src = half.acc2.at[k * 8 + mask // 2]
            slot = k * 15 + mask - 1
            copy = remote(
                src, landing(k, s, mask ^ (1 << s)), half.rs_send.at[s // 2], half.rs_recv.at[slot],
                near[(k + s) % 4],
            )
            copy.start()
            copies[k, mask] = copy

        def urgency(mask):
            rest = mask & ~1
            return (first_step(rest) if rest else 4, -mask)

        for mask in sorted((m for m in range(16) if m & 1), key=urgency):
            for k in range(STREAMS):
                send(k, mask)
        entries = sorted((m for m in range(16) if not m & 1), key=lambda m: (first_step(m) if m else 4, -m))
        for mask in entries:
            steps = first_step(mask) if mask else 4
            for k in range(STREAMS):
                at[steps - 1] += flow
                yield at[steps - 1]
                value = half.part2[block_at(k, mask), :].astype(F32)
                for s in range(steps):
                    copies[k, mask | 1 << s].wait_recv()
                    value = value + landing(k, s, mask)[...].astype(F32)
                if mask:
                    half.acc2[k * 8 + mask // 2] = value
                    send(k, mask)
                else:
                    ns_ref[pl.ds(k * Q, Q), pl.ds(lane, H)] = value

    def prepare():
        yield 0.5
        for half in halves:
            half.acc[0] = jnp.zeros((TILE, H), F32)
        plan[True] = places(cols_ref)
        plan[False] = places(rows_ref)

    def early(start, plane_at, line_at, eliminate_at):
        yield start
        rows = ns_ref[:, :H]
        shared.early_part[...] = lax.dot_general(
            rows, rows, (((0,), (0,)), ((), ())), precision=HI, preferred_element_type=F32
        )
        mine = rows_at(me * 8, 8, 8)
        for d, p in enumerate(plane):
            copy = remote(
                shared.early_part.at[rows_at(p * 8, 8, 8), :], shared.early_in.at[d],
                shared.early_send.at[0], shared.early_recv.at[0], (row, p),
            )
            copy.start()
        yield plane_at
        total = shared.early_part[mine, :]
        landed_all(shared.early_in.at[pl.ds(0, 15)], shared.early_recv.at[0])
        for d in range(15):
            total = total + shared.early_in[d]
        shared.early_slab[...] = total
        shared.early_row[row] = total
        for d, device in enumerate(line):
            copy = remote(
                shared.early_slab, shared.early_row.at[row],
                shared.early_send.at[1], shared.early_recv.at[1], device,
            )
            copy.start()
        yield line_at
        landed_all(shared.early_in.at[pl.ds(0, 15)], shared.early_recv.at[1])
        total = shared.early_row[0]
        for d in range(1, 16):
            total = total + shared.early_row[d]
        total = total * (1.0 / ROWS)
        shared.early_sum[...] = total
        shared.early_gram[mine, :] = total
        for d, p in enumerate(plane):
            copy = remote(
                shared.early_sum, shared.early_gram.at[mine, :],
                shared.early_send.at[2], shared.early_recv.at[2], (row, p),
            )
            copy.start()
        yield eliminate_at
        landed_all(shared.early_in.at[pl.ds(0, 15)], shared.early_recv.at[2])
        i0 = lax.broadcasted_iota(jnp.int32, (H, H), 0)
        i1 = lax.broadcasted_iota(jnp.int32, (H, H), 1)
        shared.work[:, :H] = shared.early_gram[...]
        shared.work[:, H:] = (i0 == i1).astype(F32)
        for n, _ in enumerate(eliminate(shared.work)):
            yield eliminate_at + (0 if n < 12 else 4.2)
        early_ref[:, :H] = jnp.where(i1 >= i0, shared.work[:, :H], 0.0)
        early_ref[:, H:] = jnp.where(i0 >= i1, shared.work[:, H:], 0.0)

    def late(start):
        yield start
        shared.late_part[...] = lax.dot_general(
            ns_ref[...], ns_ref[:, H:], (((0,), (0,)), ((), ())), precision=HI, preferred_element_type=F32
        )
        mine = rows_at(me * 16 + core * 8, 8, 8)
        for n, (r, p) in enumerate(everyone):
            theirs = rows_at(p * 16 + lax.rem(r, 2) * 8, 8, 8)
            copy = remote(
                shared.late_part.at[theirs, :], shared.slabs.at[n],
                shared.slab_send.at[0], shared.slab_recv.at[0], (r, p),
            )
            copy.start()
        yield start + 5
        total = shared.late_part[mine, :]
        landed_all(shared.slabs, shared.slab_recv.at[0])
        for n in range(31):
            total = total + shared.slabs[n]
        shared.slab[...] = total
        for d, device in enumerate(column):
            copy = remote(shared.slab, shared.z_in.at[z], shared.z_send.at[0], shared.z_recv.at[0], device)
            copy.start()
        shared.z_in[z] = total
        yield start + 9
        landed_all(shared.z_in.at[pl.ds(0, 7)], shared.z_recv.at[0])
        total = shared.z_in[0]
        for d in range(1, 8):
            total = total + shared.z_in[d]
        late_ref[mine, :] = total * (1.0 / ROWS)
        for n, device in enumerate(everyone):
            copy = remote(
                late_ref.at[mine, :], late_ref.at[mine, :], shared.out_send.at[0], shared.out_recv.at[0], device
            )
            copy.start()
        yield start + 14
        landed_all(shared.slabs, shared.out_recv.at[0])

    a, b = halves

    def first():
        yield from gather(a, 0.0, 12.5)
        yield from multiply(a, True, a.gathered, a.part, 16.0, 0.36)
        yield from exchange(a, 23.0, (23.5, 29.0, 34.6, 40.0), 46.0, (49.0, 52.0, 55.5, 59.0), 61.4)
        yield from multiply(a, False, a.columns, a.part2, 62.0, 0.3)
        yield from reduce(a, 0, 68.0, [70.5, 79.2, 82.4, 87.5], 0.1)
        yield from early(88.2, 93.4, 97.6, 102.7)

    def second():
        yield 9.0
        yield from gather(b, 13.2, 10.0)
        yield from multiply(b, True, b.gathered, b.part, 27.0, 0.36)
        yield from exchange(b, 34.0, (34.2, 42.6, 50.2, 57.0), 61.6, (64.5, 67.8, 71.2, 74.6), 77.4)
        yield from multiply(b, False, b.columns, b.part2, 78.0, 0.3)
        yield from reduce(b, H, 84.0, [87.0, 90.5, 93.5, 95.5], 0.2)
        yield from late(97.5)

    interleave([first(), prepare(), second()])
    for half in halves:
        left_all(half.gathered.at[pl.ds(0, 15 * SHARD // UNIT)], half.ag_send.at[0])
        left_all(half.pair_buf, half.pair_send.at[0])
        left_all(half.sums, half.chain_send.at[0])
        left_all(half.columns.at[pl.ds(0, 7 * PARTS * PU)], half.gather_send.at[0])
        left_all(half.columns.at[pl.ds(0, 8 * PARTS * PU)], half.twin_send.at[0])
        left_all(half.columns.at[pl.ds(0, 12 * STREAMS * PU)], half.rs_send.at[0])
        left_all(half.acc2.at[pl.ds(0, 3 * STREAMS)], half.rs_send.at[1])
    for n in range(3):
        left_all(shared.early_in.at[pl.ds(0, 15)], shared.early_send.at[n])
    left_all(shared.slabs, shared.slab_send.at[0])
    left_all(shared.z_in.at[pl.ds(0, 7)], shared.z_send.at[0])
    left_all(shared.slabs, shared.out_send.at[0])


def iterate_call(tiles, rows, cols, count, sketch):
    smem = pl.BlockSpec(memory_space=pltpu.SMEM)
    scratch = [make() for _ in range(2) for make in HALF_SCRATCH.values()]
    scratch += [make() for make in SHARED_SCRATCH.values()]
    return pl.pallas_call(
        iterate,
        out_shape=(
            jax.ShapeDtypeStruct((SHARD, K), F32),
            jax.ShapeDtypeStruct((H, K), F32),
            jax.ShapeDtypeStruct((K, H), F32),
        ),
        in_specs=[smem, smem, smem, pl.BlockSpec(memory_space=pl.ANY), whole()],
        out_specs=(whole(), whole(), whole()),
        scratch_shapes=scratch,
        compiler_params=pltpu.CompilerParams(
            collective_id=0, has_side_effects=True, vmem_limit_bytes=VMEM_LIMIT
        ),
        name="iterate",
    )(rows, cols, count, tiles, sketch)


def factor_kernel(early_ref, late_ref, ns_ref, basis_ref, factor_ref, work):
    inverse_t = early_ref[:, H:]
    across = matmul(inverse_t, late_ref[:H, :], ((1,), (0,)))
    i0 = lax.broadcasted_iota(jnp.int32, (H, H), 0)
    i1 = lax.broadcasted_iota(jnp.int32, (H, H), 1)
    work[:, :H] = late_ref[H:, :] - matmul(across, across, ((0,), (0,)))
    work[:, H:] = (i0 == i1).astype(F32)
    factor_ref[:H, :H] = early_ref[:, :H]
    factor_ref[:H, H:] = across
    factor_ref[H:, :H] = jnp.zeros((H, H), F32)
    left = matmul(ns_ref[:, :H], inverse_t, ((1,), (1,)))
    basis_ref[:, :H] = left
    rest = ns_ref[:, H:] - matmul(left, across, ((1,), (0,)))
    for _ in eliminate(work):
        pass
    factor_ref[H:, H:] = jnp.where(i1 >= i0, work[:, :H], 0.0)
    basis_ref[:, H:] = matmul(rest, jnp.where(i0 >= i1, work[:, H:], 0.0), ((1,), (1,)))


def factor_and_basis(early, late, ns):
    return pl.pallas_call(
        factor_kernel,
        out_shape=(
            jax.ShapeDtypeStruct((SHARD, K), F32),
            jax.ShapeDtypeStruct((K, K), F32),
        ),
        in_specs=[whole(), whole(), whole()],
        out_specs=(whole(), whole()),
        scratch_shapes=[vmem((H, 2 * H), F32)],
        compiler_params=pltpu.CompilerParams(vmem_limit_bytes=VMEM_LIMIT),
        name="factor",
    )(early, late, ns)


def body(tiles, tile_rows, tile_cols, tile_counts, sketch):
    ns, early, late = iterate_call(tiles[0, 0], tile_rows[0, 0], tile_cols[0, 0], tile_counts[0], sketch)
    return factor_and_basis(early, late, ns)


def solution(mesh):
    return jax.shard_map(
        body,
        mesh=mesh,
        in_specs=(
            P("row", "col", None, None, None),
            P("row", "col", None),
            P("row", "col", None),
            P("row", "col"),
            P(("row", "col"), None),
        ),
        out_specs=(P(("row", "col"), None), P()),
        check_vma=False,
    )
```

```python
import functools
import heapq

import jax
import jax.numpy as jnp
from jax import lax
from jax.experimental import pallas as pl
from jax.experimental.pallas import tpu as pltpu
from jax.sharding import PartitionSpec as P

TILE = 512
K = 256
H = 128
BR = 12
BC = 12
CAP = 16
SHARD = 384
FULL = 6144
UNIT = 32
TU = TILE // UNIT
PU = 96 // UNIT
ROWS = 98304
STREAMS = 4
Q = SHARD // STREAMS
MESH = pl.DeviceIdType.MESH
HI = lax.Precision.HIGHEST
VMEM_LIMIT = 60 * 1024 * 1024
F32 = jnp.float32
BF16 = jnp.bfloat16
PARTS = 4
PART = SHARD // PARTS
CHAINS = tuple((1 - 2 * (p % 2), p, 4) for p in range(PARTS)) + tuple((2 * (p % 2) - 1, p, 3) for p in range(PARTS))
WIRE = (BF16, BF16, F32, F32)


def vmem(shape, dtype):
    return pltpu.VMEM(shape, dtype)


def dma(n):
    return pltpu.SemaphoreType.DMA((n,))


def whole():
    return pl.BlockSpec(memory_space=pltpu.VMEM)


def flip(i, g):
    x, y = lax.rem(i, 4), lax.div(i, 4)
    if g == 0:
        return i + 1 - 2 * lax.rem(x, 2)
    if g == 1:
        return i + 3 - 2 * x
    if g == 2:
        return i + 4 - 8 * lax.rem(y, 2)
    return i + 12 - 8 * y


def rows_at(start, size, step):
    return pl.ds(pl.multiple_of(start, step), size)


def remote(src, dst, send_sem, recv_sem, device):
    return pltpu.make_async_remote_copy(
        src_ref=src,
        dst_ref=dst,
        send_sem=send_sem,
        recv_sem=recv_sem,
        device_id=device,
        device_id_type=MESH,
    )


def last_step(mask):
    return mask.bit_length() - 1


def first_step(mask):
    return (mask & -mask).bit_length() - 1


def slot_of(n, t):
    return n * 4 + t - 1 if n < PARTS else PARTS * 4 + (n - PARTS) * 3 + t - 1


def interleave(processes):
    queue = []
    for n, process in enumerate(processes):
        heapq.heappush(queue, (next(process), n, process))
    while queue:
        _, n, process = heapq.heappop(queue)
        try:
            heapq.heappush(queue, (next(process), n, process))
        except StopIteration:
            pass


def wide(x):
    return jnp.broadcast_to(x, (8, H))


def matmul(a, b, contract):
    return lax.dot_general(a, b, (contract, ((), ())), precision=HI, preferred_element_type=F32)


def eliminate(work):
    sub = lax.broadcasted_iota(jnp.int32, (8, H), 0)
    panels = H // 8
    below = None
    for p in range(panels):
        j = p * 8
        parts = [work[pl.ds(j, 8), :H], work[pl.ds(j, 8), H:]] if below is None else below
        cols = [wide(parts[0][:, j + k : j + k + 1]) for k in range(8)]
        below = None
        if p + 1 < panels:
            m = j + 8
            rows = work[pl.ds(m, 8), :]
            if p:
                done = work[pl.ds(0, j), :]
                rows = rows - matmul(done[:, m : m + 8], done, ((0,), (0,)))
            below = [rows[:, :H], rows[:, H:]]
            under = [wide(below[0][:, j + k : j + k + 1]) for k in range(8)]
        for i in range(8):
            scale = lax.rsqrt(wide(cols[i][i : i + 1, :]))
            down = jnp.where(sub > i, cols[i] * scale, 0.0)
            if below is not None:
                drop = under[i] * scale
            for k in range(i + 1, 8):
                line = wide(cols[k][i : i + 1, :]) * scale
                cols[k] = cols[k] - down * line
                if below is not None:
                    under[k] = under[k] - drop * line
            for q in range(2):
                line = wide(parts[q][i : i + 1, :]) * scale
                parts[q] = jnp.where(sub == i, line, parts[q] - down * line)
                if below is not None:
                    below[q] = below[q] - drop * line
        for q in range(2):
            work[pl.ds(j, 8), q * H : (q + 1) * H] = parts[q]
        yield


HALF_SCRATCH = dict(
    shard=lambda: vmem((SHARD // UNIT, UNIT, H), BF16),
    gathered=lambda: vmem((FULL // UNIT, UNIT, H), BF16),
    ag_send=lambda: dma(1),
    ag_recv=lambda: dma(STREAMS * 15),
    acc=lambda: vmem((CAP + 1, TILE, H), F32),
    part=lambda: vmem((FULL, H), F32),
    pair_buf=lambda: vmem((8 * PARTS, PART, H), F32),
    sums=lambda: vmem((7 * PARTS, PART, H), F32),
    landed=lambda: vmem((7 * PARTS, PART, H), F32),
    pair_send=lambda: dma(1),
    pair_recv=lambda: dma(8 * PARTS),
    chain_send=lambda: dma(1),
    chain_recv=lambda: dma(7 * PARTS),
    own=lambda: vmem((SHARD // UNIT, UNIT, H), BF16),
    columns=lambda: vmem((FULL // UNIT, UNIT, H), BF16),
    gather_send=lambda: dma(1),
    gather_recv=lambda: dma(7 * PARTS),
    twin_send=lambda: dma(1),
    twin_recv=lambda: dma(1),
    part2=lambda: vmem((FULL, H), BF16),
    land0=lambda: vmem((STREAMS * 8, Q, H), BF16),
    land1=lambda: vmem((STREAMS * 4, Q, H), WIRE[1]),
    land2=lambda: vmem((STREAMS * 3, Q, H), F32),
    acc2=lambda: vmem((STREAMS * 8, Q, H), F32),
    wire1=lambda: vmem((STREAMS * 4, Q, H), BF16),
    rs_send=lambda: dma(2),
    rs_recv=lambda: dma(STREAMS * 15),
)

SHARED_SCRATCH = dict(
    tiles=lambda: vmem((CAP, TILE, TILE), BF16),
    tile_sem=lambda: dma(CAP),
    work=lambda: vmem((H, 2 * H), F32),
    early_part=lambda: vmem((H, H), F32),
    early_in=lambda: vmem((16, 8, H), F32),
    early_row=lambda: vmem((16, 8, H), F32),
    early_slab=lambda: vmem((8, H), F32),
    early_sum=lambda: vmem((8, H), F32),
    early_gram=lambda: vmem((H, H), F32),
    early_send=lambda: dma(3),
    early_recv=lambda: dma(3),
    late_part=lambda: vmem((K, H), F32),
    slabs=lambda: vmem((31, 8, H), F32),
    slab=lambda: vmem((8, H), F32),
    slab_send=lambda: dma(1),
    slab_recv=lambda: dma(1),
    z_in=lambda: vmem((8, 8, H), F32),
    z_send=lambda: dma(1),
    z_recv=lambda: dma(1),
    out_send=lambda: dma(1),
    out_recv=lambda: dma(1),
)


class Refs:
    pass


def named(names, refs):
    out = Refs()
    for name, ref in zip(names, refs):
        setattr(out, name, ref)
    return out


def iterate(rows_ref, cols_ref, count_ref, tiles_ref, sketch_ref, ns_ref, early_ref, late_ref, *scratch):
    nh = len(HALF_SCRATCH)
    halves = [named(HALF_SCRATCH, scratch[i * nh : (i + 1) * nh]) for i in (0, 1)]
    shared = named(SHARED_SCRATCH, scratch[2 * nh :])

    row, me = lax.axis_index("row"), lax.axis_index("col")
    z, core = lax.div(row, 2), lax.rem(row, 2)
    other = row + 1 - 2 * core
    twin = (other, me)
    near = [(row, flip(me, g)) for g in range(4)]
    plane = [lax.rem(me + d, 16) for d in range(1, 16)]

    def ring(d):
        return lax.rem(z + d + 8, 8)

    side = {1: (2 * ring(1) + core, me), -1: (2 * ring(-1) + core, me)}
    column = [(2 * ring(d) + core, me) for d in range(1, 8)]
    everyone = [twin] + [(r, p) for p in plane for r in (row, other)]
    line = [(lax.rem(row + d, 16), me) for d in range(1, 16)]

    loads = []
    for s in range(CAP):
        load = pltpu.make_async_copy(tiles_ref.at[s], shared.tiles.at[s], shared.tile_sem.at[s])
        load.start()
        loads.append(load)
    for i, half in enumerate(halves):
        half.shard[...] = sketch_ref[:, i * H : (i + 1) * H].reshape(SHARD // UNIT, UNIT, H)

    barrier = pltpu.get_barrier_semaphore()
    greeted = everyone[1:] + line
    for device in greeted:
        pl.semaphore_signal(barrier, inc=1, device_id=device, device_id_type=MESH)
    pl.semaphore_wait(barrier, len(greeted))

    plan = {}

    def landed_all(view, sem):
        remote(view, view, sem, sem, twin).wait_recv()

    def left_all(view, sem):
        remote(view, view, sem, sem, twin).wait_send()

    def places(targets):
        to = [targets[t] for t in range(CAP)]
        count = count_ref[0]
        before, ends = [], []
        for s in range(CAP):
            at = jnp.int32(0)
            for t in range(s):
                at = jnp.where(to[t] == to[s], t + 1, at)
            before.append(at)
        for b in range(BR):
            at = jnp.int32(0)
            for t in range(CAP):
                at = jnp.where((to[t] == b) & (t < count), t + 1, at)
            ends.append(at)
        return before, ends

    def gather(half, start, flow, merged=False):
        copies = {}
        half.gathered[pl.ds(me * (SHARD // UNIT), SHARD // UNIT)] = half.shard[...]

        def block_at(k, mask):
            block = me
            for s in range(4):
                if mask >> s & 1:
                    block = flip(block, (k + s) % 4)
            return pl.ds(block * (SHARD // UNIT) + k * (Q // UNIT), Q // UNIT)

        def forward(k, mask, s):
            at = block_at(k, mask)
            src = half.shard.at[pl.ds(k * (Q // UNIT), Q // UNIT)] if mask == 0 else half.gathered.at[at]
            slot = k * 15 + (mask | 1 << s) - 1
            copy = remote(
                src, half.gathered.at[at], half.ag_send.at[0],
                half.ag_recv.at[slot % 15 if merged else slot], near[(k + s) % 4]
            )
            copy.start()
            copies[k, mask | 1 << s] = copy

        for s in range(4):
            for k in range(STREAMS):
                forward(k, 0, s)
        masks = sorted(range(1, 16), key=lambda m: (m.bit_count(), last_step(m), m))
        n = 0
        for mask in masks:
            for k in range(STREAMS):
                yield start + 3 + flow * n / 60
                n += 1
                if not merged:
                    copies[k, mask].wait_recv()
                elif k == 0:
                    landed_all(half.gathered.at[pl.ds(0, STREAMS * PU)], half.ag_recv.at[mask - 1])
                for s in range(last_step(mask) + 1, 4):
                    forward(k, mask, s)

    def multiply(half, transposed, source, result, start, per_tile):
        src = rows_ref if transposed else cols_ref
        before, ends = plan[transposed]
        dims = (((0,), (0,)), ((), ())) if transposed else (((1,), (0,)), ((), ()))
        for s in range(CAP):
            yield start + per_tile * s
            if loads[s] is not None:
                loads[s].wait()
                loads[s] = None
            block = source[pl.ds(src[s] * TU, TU)].reshape(TILE, H)
            for u in range(2):
                part = pl.ds(u * 256, 256)
                tile = shared.tiles[s, :, part] if transposed else shared.tiles[s, part, :]
                half.acc[s + 1, part, :] = half.acc[before[s], part, :] + lax.dot_general(
                    tile, block, dims, preferred_element_type=F32
                )
        for b in range(BR):
            yield start + per_tile * CAP + 0.08 * b
            result[pl.ds(b * TILE, TILE), :] = half.acc[ends[b]].astype(result.dtype)

    def exchange(half, start, reduce_at, own_at, gather_at, twins_at):
        yield start
        order = []
        for t in range(1, 5):
            for direction, part, hops in CHAINS:
                if t <= hops:
                    item = (direction * (hops + 1 - t) % 8, part)
                    if item not in order:
                        order.append(item)
        order += [(0, part) for part in range(PARTS)]
        pair = {}
        for d, part in order:
            slot = d * PARTS + part
            theirs = rows_at((2 * ring(d) + 1 - core) * SHARD + part * PART, PART, PART)
            pair[d, part] = remote(
                half.part.at[theirs, :], half.pair_buf.at[slot],
                half.pair_send.at[0], half.pair_recv.at[slot], twin,
            )
            pair[d, part].start()
        arrived = set()

        def chip_sum(d, part):
            d = d % 8
            slot = d * PARTS + part
            if (d, part) not in arrived:
                pair[d, part].wait_recv()
                arrived.add((d, part))
            mine = rows_at((2 * ring(d) + core) * SHARD + part * PART, PART, PART)
            return half.part[mine, :] + half.pair_buf[slot]

        last = {}
        for t in range(1, 5):
            for n, (direction, part, hops) in enumerate(CHAINS):
                if t > hops:
                    continue
                yield reduce_at[t - 1] + 0.3 * n
                slot = slot_of(n, t)
                value = chip_sum(direction * (hops + 1 - t), part)
                if t > 1:
                    last[n].wait_recv()
                    value = value + half.landed[slot - 1]
                half.sums[slot] = value
                copy = remote(
                    half.sums.at[slot], half.landed.at[slot],
                    half.chain_send.at[0], half.chain_recv.at[slot], side[direction],
                )
                copy.start()
                last[n] = copy
        moving = {}

        def spread(src, at):
            copy = remote(src, half.columns.at[at], half.twin_send.at[0], half.twin_recv.at[0], twin)
            copy.start()

        def pass_on(src, at, n, t):
            slot = slot_of(n, t + 1)
            copy = remote(
                src, half.columns.at[at],
                half.gather_send.at[0], half.gather_recv.at[slot], side[CHAINS[n][0]],
            )
            copy.start()
            moving[n] = copy

        for part in range(PARTS):
            yield own_at + 0.02 * part
            value = chip_sum(0, part)
            for n in (part + PARTS, part):
                last[n].wait_recv()
                value = value + half.landed[slot_of(n, CHAINS[n][2])]
            local = pl.ds(part * PU, PU)
            rounded = value.astype(BF16).reshape(PU, UNIT, H)
            half.own[local] = rounded
            at = pl.ds((row * PARTS + part) * PU, PU)
            half.columns[at] = rounded
            for n in range(2 * PARTS):
                if CHAINS[n][1] == part:
                    pass_on(half.own.at[local], at, n, 0)
            spread(half.own.at[local], at)
        for t in range(1, 5):
            for n, (direction, part, hops) in enumerate(CHAINS):
                if t > hops:
                    continue
                yield gather_at[t - 1] + 0.3 * n
                moving[n].wait_recv()
                at = pl.ds(((2 * ring(-direction * t) + core) * PARTS + part) * PU, PU)
                if t < hops:
                    pass_on(half.columns.at[at], at, n, t)
                spread(half.columns.at[at], at)
        yield twins_at
        landed_all(half.columns.at[pl.ds(0, 8 * PARTS * PU)], half.twin_recv.at[0])

    def reduce(half, lane, start, at, flow):
        yield start
        copies = {}

        def block_at(k, mask):
            block = me
            for s in range(4):
                if mask >> s & 1:
                    block = flip(block, (k + s) % 4)
            return rows_at(block * SHARD + k * Q, Q, 16)

        def landing(k, s, mask):
            if s == 0:
                return half.land0.at[k * 8 + mask // 2]
            if s == 1:
                return half.land1.at[k * 4 + mask // 4]
            return half.land2.at[k * 3 + (mask // 8 if s == 2 else 2)]

        def send(k, mask):
            s = first_step(mask)
            if s == 0:
                src = half.part2.at[block_at(k, mask), :]
            elif WIRE[s] == BF16:
                half.wire1[k * 4 + mask // 4] = half.acc2[k * 8 + mask // 2].astype(BF16)
                src = half.wire1.at[k * 4 + mask // 4]
            else:
                src = half.acc2.at[k * 8 + mask // 2]
            slot = k * 15 + mask - 1
            copy = remote(
                src, landing(k, s, mask ^ (1 << s)), half.rs_send.at[s // 2], half.rs_recv.at[slot],
                near[(k + s) % 4],
            )
            copy.start()
            copies[k, mask] = copy

        def urgency(mask):
            rest = mask & ~1
            return (first_step(rest) if rest else 4, -mask)

        for mask in sorted((m for m in range(16) if m & 1), key=urgency):
            for k in range(STREAMS):
                send(k, mask)
        entries = sorted((m for m in range(16) if not m & 1), key=lambda m: (first_step(m) if m else 4, -m))
        for mask in entries:
            steps = first_step(mask) if mask else 4
            for k in range(STREAMS):
                at[steps - 1] += flow
                yield at[steps - 1]
                value = half.part2[block_at(k, mask), :].astype(F32)
                for s in range(steps):
                    copies[k, mask | 1 << s].wait_recv()
                    value = value + landing(k, s, mask)[...].astype(F32)
                if mask:
                    half.acc2[k * 8 + mask // 2] = value
                    send(k, mask)
                else:
                    ns_ref[pl.ds(k * Q, Q), pl.ds(lane, H)] = value

    def prepare():
        yield 0.5
        for half in halves:
            half.acc[0] = jnp.zeros((TILE, H), F32)
        plan[True] = places(cols_ref)
        plan[False] = places(rows_ref)

    def early(start, plane_at, line_at, eliminate_at):
        yield start
        rows = ns_ref[:, :H]
        shared.early_part[...] = lax.dot_general(
            rows, rows, (((0,), (0,)), ((), ())), precision=HI, preferred_element_type=F32
        )
        mine = rows_at(me * 8, 8, 8)
        for d, p in enumerate(plane):
            copy = remote(
                shared.early_part.at[rows_at(p * 8, 8, 8), :], shared.early_in.at[d],
                shared.early_send.at[0], shared.early_recv.at[0], (row, p),
            )
            copy.start()
        yield plane_at
        total = shared.early_part[mine, :]
        landed_all(shared.early_in.at[pl.ds(0, 15)], shared.early_recv.at[0])
        for d in range(15):
            total = total + shared.early_in[d]
        shared.early_slab[...] = total
        shared.early_row[row] = total
        for d, device in enumerate(line):
            copy = remote(
                shared.early_slab, shared.early_row.at[row],
                shared.early_send.at[1], shared.early_recv.at[1], device,
            )
            copy.start()
        yield line_at
        landed_all(shared.early_in.at[pl.ds(0, 15)], shared.early_recv.at[1])
        total = shared.early_row[0]
        for d in range(1, 16):
            total = total + shared.early_row[d]
        total = total * (1.0 / ROWS)
        shared.early_sum[...] = total
        shared.early_gram[mine, :] = total
        for d, p in enumerate(plane):
            copy = remote(
                shared.early_sum, shared.early_gram.at[mine, :],
                shared.early_send.at[2], shared.early_recv.at[2], (row, p),
            )
            copy.start()
        yield eliminate_at
        landed_all(shared.early_in.at[pl.ds(0, 15)], shared.early_recv.at[2])
        i0 = lax.broadcasted_iota(jnp.int32, (H, H), 0)
        i1 = lax.broadcasted_iota(jnp.int32, (H, H), 1)
        shared.work[:, :H] = shared.early_gram[...]
        shared.work[:, H:] = (i0 == i1).astype(F32)
        for n, _ in enumerate(eliminate(shared.work)):
            yield eliminate_at + (0 if n < 9 else 4.2)
        early_ref[:, :H] = jnp.where(i1 >= i0, shared.work[:, :H], 0.0)
        early_ref[:, H:] = jnp.where(i0 >= i1, shared.work[:, H:], 0.0)

    def late(start):
        yield start
        shared.late_part[...] = lax.dot_general(
            ns_ref[...], ns_ref[:, H:], (((0,), (0,)), ((), ())), precision=HI, preferred_element_type=F32
        )
        mine = rows_at(me * 16 + core * 8, 8, 8)
        for n, (r, p) in enumerate(everyone):
            theirs = rows_at(p * 16 + lax.rem(r, 2) * 8, 8, 8)
            copy = remote(
                shared.late_part.at[theirs, :], shared.slabs.at[n],
                shared.slab_send.at[0], shared.slab_recv.at[0], (r, p),
            )
            copy.start()
        yield start + 5
        total = shared.late_part[mine, :]
        landed_all(shared.slabs, shared.slab_recv.at[0])
        for n in range(31):
            total = total + shared.slabs[n]
        shared.slab[...] = total
        for d, device in enumerate(column):
            copy = remote(shared.slab, shared.z_in.at[z], shared.z_send.at[0], shared.z_recv.at[0], device)
            copy.start()
        shared.z_in[z] = total
        yield start + 9
        landed_all(shared.z_in.at[pl.ds(0, 7)], shared.z_recv.at[0])
        total = shared.z_in[0]
        for d in range(1, 8):
            total = total + shared.z_in[d]
        late_ref[mine, :] = total * (1.0 / ROWS)
        for n, device in enumerate(everyone):
            copy = remote(
                late_ref.at[mine, :], late_ref.at[mine, :], shared.out_send.at[0], shared.out_recv.at[0], device
            )
            copy.start()
        yield start + 14
        landed_all(shared.slabs, shared.out_recv.at[0])

    a, b = halves

    def first():
        yield from gather(a, 0.0, 12.5)
        yield from multiply(a, True, a.gathered, a.part, 16.0, 0.36)
        yield from exchange(a, 23.0, (23.5, 29.0, 34.6, 40.0), 46.0, (49.0, 52.0, 55.5, 59.0), 61.4)
        yield from multiply(a, False, a.columns, a.part2, 62.0, 0.3)
        yield from reduce(a, 0, 68.0, [70.5, 79.2, 82.4, 87.5], 0.1)
        yield from early(88.2, 93.4, 97.6, 102.7)

    def second():
        yield 9.0
        yield from gather(b, 13.2, 10.0, merged=True)
        yield from multiply(b, True, b.gathered, b.part, 27.0, 0.36)
        yield from exchange(b, 34.0, (34.2, 42.6, 50.2, 57.0), 61.6, (64.5, 67.8, 71.2, 74.6), 77.4)
        yield from multiply(b, False, b.columns, b.part2, 78.0, 0.3)
        yield from reduce(b, H, 84.0, [87.0, 90.5, 93.5, 95.5], 0.2)
        yield from late(97.5)

    interleave([first(), prepare(), second()])
    for half in halves:
        left_all(half.gathered.at[pl.ds(0, 15 * SHARD // UNIT)], half.ag_send.at[0])
        left_all(half.pair_buf, half.pair_send.at[0])
        left_all(half.sums, half.chain_send.at[0])
        left_all(half.columns.at[pl.ds(0, 7 * PARTS * PU)], half.gather_send.at[0])
        left_all(half.columns.at[pl.ds(0, 8 * PARTS * PU)], half.twin_send.at[0])
        left_all(half.columns.at[pl.ds(0, 12 * STREAMS * PU)], half.rs_send.at[0])
        left_all(half.acc2.at[pl.ds(0, 3 * STREAMS)], half.rs_send.at[1])
    for n in range(3):
        left_all(shared.early_in.at[pl.ds(0, 15)], shared.early_send.at[n])
    left_all(shared.slabs, shared.slab_send.at[0])
    left_all(shared.z_in.at[pl.ds(0, 7)], shared.z_send.at[0])
    left_all(shared.slabs, shared.out_send.at[0])


def iterate_call(tiles, rows, cols, count, sketch):
    smem = pl.BlockSpec(memory_space=pltpu.SMEM)
    scratch = [make() for make in HALF_SCRATCH.values()]
    scratch += [dma(15) if name == "ag_recv" else make() for name, make in HALF_SCRATCH.items()]
    scratch += [make() for make in SHARED_SCRATCH.values()]
    return pl.pallas_call(
        iterate,
        out_shape=(
            jax.ShapeDtypeStruct((SHARD, K), F32),
            jax.ShapeDtypeStruct((H, K), F32),
            jax.ShapeDtypeStruct((K, H), F32),
        ),
        in_specs=[smem, smem, smem, pl.BlockSpec(memory_space=pl.ANY), whole()],
        out_specs=(whole(), whole(), whole()),
        scratch_shapes=scratch,
        compiler_params=pltpu.CompilerParams(
            collective_id=0, has_side_effects=True, vmem_limit_bytes=VMEM_LIMIT
        ),
        name="iterate",
    )(rows, cols, count, tiles, sketch)


def factor_kernel(early_ref, late_ref, ns_ref, basis_ref, factor_ref, work):
    inverse_t = early_ref[:, H:]
    across = matmul(inverse_t, late_ref[:H, :], ((1,), (0,)))
    i0 = lax.broadcasted_iota(jnp.int32, (H, H), 0)
    i1 = lax.broadcasted_iota(jnp.int32, (H, H), 1)
    work[:, :H] = late_ref[H:, :] - matmul(across, across, ((0,), (0,)))
    work[:, H:] = (i0 == i1).astype(F32)
    factor_ref[:H, :H] = early_ref[:, :H]
    factor_ref[:H, H:] = across
    factor_ref[H:, :H] = jnp.zeros((H, H), F32)
    left = matmul(ns_ref[:, :H], inverse_t, ((1,), (1,)))
    basis_ref[:, :H] = left
    rest = ns_ref[:, H:] - matmul(left, across, ((1,), (0,)))
    for _ in eliminate(work):
        pass
    factor_ref[H:, H:] = jnp.where(i1 >= i0, work[:, :H], 0.0)
    basis_ref[:, H:] = matmul(rest, jnp.where(i0 >= i1, work[:, H:], 0.0), ((1,), (1,)))


def factor_and_basis(early, late, ns):
    return pl.pallas_call(
        factor_kernel,
        out_shape=(
            jax.ShapeDtypeStruct((SHARD, K), F32),
            jax.ShapeDtypeStruct((K, K), F32),
        ),
        in_specs=[whole(), whole(), whole()],
        out_specs=(whole(), whole()),
        scratch_shapes=[vmem((H, 2 * H), F32)],
        compiler_params=pltpu.CompilerParams(vmem_limit_bytes=VMEM_LIMIT),
        name="factor",
    )(early, late, ns)


def body(tiles, tile_rows, tile_cols, tile_counts, sketch):
    ns, early, late = iterate_call(tiles[0, 0], tile_rows[0, 0], tile_cols[0, 0], tile_counts[0], sketch)
    return factor_and_basis(early, late, ns)


def solution(mesh):
    return jax.shard_map(
        body,
        mesh=mesh,
        in_specs=(
            P("row", "col", None, None, None),
            P("row", "col", None),
            P("row", "col", None),
            P("row", "col"),
            P(("row", "col"), None),
        ),
        out_specs=(P(("row", "col"), None), P()),
        check_vma=False,
    )
```
